256 devices in a mesh: gx: 4 (over y), gy: 8 (over x, core), gz: 8 (over z).
Axes of the slice: x: 4, y: 4, z: 8, core: 2. Of those that a mesh axis runs over, the one named last changes fastest.
Arguments:
- field: float32 [4, 16384, 512], P(None, ('gx', 'gy', 'gz')), may hold values from -6 to 6
- neighbours: int32 [16384, 6], P(('gx', 'gy', 'gz')), may hold values from -1 to 16383, as said below
- cell_one: int32 [524288], P(('gx', 'gy', 'gz')), may hold values from 0 to 16383, as said below
- ref_one: float32 [3, 524288], P(None, ('gx', 'gy', 'gz')), may hold values from -1 to 1
- cell_two: int32 [524288], P(('gx', 'gy', 'gz')), may hold values from 0 to 16383, as said below
- ref_two: float32 [3, 524288], P(None, ('gx', 'gy', 'gz')), may hold values from -1 to 1
- velocity: float32 [3, 524288], P(None, ('gx', 'gy', 'gz')), may hold values from -6 to 6
- rate: float32 [524288], P(('gx', 'gy', 'gz')), may hold values from 0.5 to 8
- cut: int32 [1], replicated, may hold values from 1 to 2047
Outputs:
- field_out: float32 [4, 16384, 512], P(None, ('gx', 'gy', 'gz'))
- velocity_out: float32 [3, 524288], P(None, ('gx', 'gy', 'gz'))
The draws below stay inside these ranges and needn't reach their ends.
Inputs may be any that keep to these rules, and one draw needn't show every extreme that they name: `neighbours`: across face f of an element lies an element of the same device or of the adjacent device along that face's axis (cyclic along gz), with the same face node order; -1 marks walls at the ends along gx and gy. The order of elements within a device is arbitrary. `cell_one`: A particle's element is owned by a device with the same gx index as its bin. From one bin at most 64 particles lie in the elements of one device, and in each slab one device receives exactly 64 from every bin of the slab. `cell_two`: as for cell_one, for the second step's bins.
All inputs are finite; a program needn't handle non-finite values.
Results may differ from the reference program's by a relative error of at most 0.0003.
Values sent between devices are 32-bit elements; how exact they have to be, the bound alone decides.
No kernel may reach another device: no remote copies, remote signals or barrier semaphores. Data moves between devices by JAX's collectives and lax.ppermute only.
A program may use at most 128 MiB of HBM per device.

```python
import math
import jax
import jax.numpy as jnp
import numpy as np
from jax import lax

NODES = 8
EDGE = 4
BIN = 2048
ELEMS = 16384
PARTICLES = 524288
N_GX = 4
N_GY = 8
N_GZ = 8
DEVICES = 256


def draw_neighbours(key, part):
    elements = EDGE * EDGE * EDGE
    orders = jax.vmap(lambda item_key: jax.random.permutation(item_key, elements))(jax.random.split(jax.random.fold_in(key, 5), DEVICES)).astype(jnp.int32)
    slot_at = jnp.argsort(orders, axis=1).astype(jnp.int32)
    device = jnp.arange(DEVICES, dtype=jnp.int32)[:, None]
    block_x = device // (N_GY * N_GZ)
    block_y = device // N_GZ % N_GY
    block_z = device % N_GZ
    coord_x = block_x * EDGE + orders // (EDGE * EDGE)
    coord_y = block_y * EDGE + orders // EDGE % EDGE
    coord_z = block_z * EDGE + orders % EDGE
    spans = (N_GX * EDGE, N_GY * EDGE, N_GZ * EDGE)
    columns = []
    for axis_index in range(3):
        for step_sign in (-1, 1):
            moved = [coord_x, coord_y, coord_z]
            shifted = moved[axis_index] + step_sign
            if axis_index == 2:
                inside = shifted == shifted
                shifted = shifted % spans[2]
            else:
                inside = (shifted >= 0) & (shifted < spans[axis_index])
                shifted = jnp.clip(shifted, 0, spans[axis_index] - 1)
            moved[axis_index] = shifted
            target_device = (moved[0] // EDGE * N_GY + moved[1] // EDGE) * N_GZ + moved[2] // EDGE
            target_position = (moved[0] % EDGE * EDGE + moved[1] % EDGE) * EDGE + moved[2] % EDGE
            target_slot = slot_at[target_device, target_position]
            columns.append(jnp.where(inside, target_device * elements + target_slot, -1))
    return jnp.stack(columns, axis=-1).reshape(DEVICES * elements, 6).astype(jnp.int32)


def particle_cells(key):
    owners = N_GY * N_GZ
    mean = BIN // owners
    capacity = 2 * mean
    elements = EDGE * EDGE * EDGE
    pattern = np.array([capacity] * (owners // 4) + [3 * mean // 4] * (owners // 2) + [mean // 2] * (owners // 4))
    bounds = jnp.asarray(np.cumsum(pattern), jnp.int32)
    special_key, bin_key = jax.random.split(key)
    special = jax.random.randint(special_key, (N_GX,), 0, owners).astype(jnp.int32)

    def one_bin(item_key, device):
        first_key, second_key, third_key = jax.random.split(item_key, 3)
        others = jax.random.permutation(first_key, owners - 1).astype(jnp.int32)
        slab = device // owners
        leader = special[slab]
        entry_owner = jnp.concatenate([leader[None], (leader + 1 + others) % owners])
        shuffled = jax.random.permutation(second_key, BIN).astype(jnp.int32)
        entry = jnp.searchsorted(bounds, shuffled, side='right').astype(jnp.int32)
        owner = entry_owner[entry]
        element = jax.random.randint(third_key, (BIN,), 0, elements).astype(jnp.int32)
        return (slab * owners + owner) * elements + element
    cells = jax.vmap(one_bin)(jax.random.split(bin_key, DEVICES), jnp.arange(DEVICES, dtype=jnp.int32))
    return cells.reshape(-1).astype(jnp.int32)


def draw_cell_one(key, part):
    return particle_cells(jax.random.fold_in(key, 11))


def draw_cell_two(key, part):
    return particle_cells(jax.random.fold_in(key, 23))


def levels(own_key, dims, cuts, smallest, high):
    loudness, own = 1.0, jax.random.fold_in(own_key, 6)
    for dim, blocks in cuts:
        heights = jnp.exp(jax.random.uniform(jax.random.fold_in(own, dim), (blocks,), jnp.float32, smallest / len(cuts), high / len(cuts)))
        loudness = loudness * jnp.repeat(heights, dims[dim] // blocks).reshape([-1 if axis == dim else 1 for axis in range(len(dims))])
    return loudness


def centred(stream_key, shape, width, bound, pieces=(), kind=jnp.bfloat16):
    values = jax.random.normal(stream_key, shape, jnp.float32) * width
    if len(pieces) > 0:
        values = levels(stream_key, shape, pieces, -0.22, 0.18) * values
    return jnp.clip(values, min=-bound, max=bound).astype(kind)


def setup_inputs(seed: int = 0) -> dict:
    streams_of = jax.random.split(jax.random.key(seed), 10)
    field = centred(streams_of[0], (4, ELEMS, NODES * NODES * NODES), 1.0, 6.0, ((1, 256),), jnp.float32)
    neighbours = draw_neighbours(jax.random.fold_in(streams_of[9], 71), 0)
    cell_one = draw_cell_one(jax.random.fold_in(streams_of[9], 71), 0)
    ref_one = jnp.clip(jax.random.uniform(streams_of[3], (3, PARTICLES), jnp.float32, -1.0, 1.0) * levels(streams_of[3], (3, PARTICLES), ((1, 256),), -0.4, 0.0), -1.0, 1.0)
    cell_two = draw_cell_two(jax.random.fold_in(streams_of[9], 71), 0)
    ref_two = jnp.clip(jax.random.uniform(streams_of[5], (3, PARTICLES), jnp.float32, -1.0, 1.0) * levels(streams_of[5], (3, PARTICLES), ((1, 256),), -0.4, 0.0), -1.0, 1.0)
    velocity = centred(streams_of[6], (3, PARTICLES), 1.0, 6.0, ((1, 256),), jnp.float32)
    rate = jnp.clip(jnp.exp(math.log(8.0) - 2.7725887 * jax.random.uniform(streams_of[7], (PARTICLES,), jnp.float32) ** levels(streams_of[7], (PARTICLES,), ((0, 256),), -0.2, 0.2)), 0.5, 8.0)
    cut = jax.random.randint(streams_of[8], (1,), 1, BIN).astype(jnp.int32)
    return dict(field=field, neighbours=neighbours, cell_one=cell_one, ref_one=ref_one, cell_two=cell_two, ref_two=ref_two, velocity=velocity, rate=rate, cut=cut)


node_points = -np.cos(np.pi * np.arange(8) / 7.0)
step_time = 0.1
viscosity = 0.002
penalty = 0.25
loading = 0.5
heating = 0.5


def gap_table():
    differences = node_points[:, None] - node_points[None, :] + np.eye(8)
    inverse = 1.0 / differences
    return inverse * (1.0 - np.eye(8))


def laplace_table():
    differences = node_points[:, None] - node_points[None, :] + np.eye(8)
    weights = 1.0 / np.prod(differences, axis=1)
    derivative = (weights[None, :] / weights[:, None]) / differences
    derivative = derivative * (1.0 - np.eye(8))
    derivative = derivative - np.eye(8) * derivative.sum(axis=1)[:, None]
    second = derivative @ derivative
    identity = np.eye(8)
    operator = np.kron(np.kron(second, identity), identity)
    operator = operator + np.kron(np.kron(identity, second), identity)
    operator = operator + np.kron(np.kron(identity, identity), second)
    return operator.T


def face_table():
    selection = np.zeros((512, 384))
    for face_side in range(6):
        edge_value = 0 if face_side % 2 == 0 else 7
        for row_node in range(8):
            for col_node in range(8):
                if face_side < 2:
                    node_index = (edge_value * 8 + row_node) * 8 + col_node
                elif face_side < 4:
                    node_index = (row_node * 8 + edge_value) * 8 + col_node
                else:
                    node_index = (row_node * 8 + col_node) * 8 + edge_value
                selection[node_index, face_side * 64 + row_node * 8 + col_node] = 1.0
    return selection


def expand_table(direction):
    positions = np.arange(512)
    digits = (positions // (8 ** (2 - direction))) % 8
    return np.where(digits[None, :] == np.arange(8)[:, None], 1.0, 0.0)


def lagrange(coordinate):
    points = jnp.asarray(node_points, jnp.float32)
    inverse = jnp.asarray(gap_table(), jnp.float32)
    identity = jnp.eye(8, dtype=jnp.float32)
    offsets = coordinate[:, None] - points[None, :]
    factors = offsets[:, None, :] * inverse[None, :, :] + identity[None, :, :]
    return jnp.prod(factors, axis=2)


def basis(coords):
    result = None
    for direction in range(3):
        spread = jnp.dot(lagrange(coords[direction]), jnp.asarray(expand_table(direction), jnp.float32), precision=lax.Precision.HIGHEST)
        result = spread if result is None else result * spread
    return result


def surface_jump(field, neighbours):
    selection = jnp.asarray(face_table(), jnp.float32)
    elements = field.shape[1]
    faces = jnp.dot(field.reshape(-1, 512), selection, precision=lax.Precision.HIGHEST).reshape(4, elements, 6, 64)
    jumps = []
    for face_side in range(6):
        target = neighbours[:, face_side]
        present = target >= 0
        partner = faces[:, jnp.maximum(target, 0), face_side ^ 1, :]
        partner = jnp.where(present[None, :, None], partner, jnp.zeros_like(partner))
        jumps.append(partner - faces[:, :, face_side, :])
    joined = jnp.stack(jumps, axis=2).reshape(-1, 384)
    return jnp.dot(joined, selection.T, precision=lax.Precision.HIGHEST).reshape(field.shape)


def fluid_step(field, neighbours, force):
    laplace = jnp.dot(field.reshape(-1, 512), jnp.asarray(laplace_table(), jnp.float32), precision=lax.Precision.HIGHEST).reshape(field.shape)
    coupling = jnp.asarray([-loading, -loading, -loading, heating], jnp.float32)
    return field + viscosity * laplace + penalty * surface_jump(field, neighbours) + coupling[:, None, None] * force


def coupled_step(field, neighbours, cells, coords, speeds, rates):
    total = cells.shape[0]
    block_size = 8192
    blocks = total // block_size
    cell_blocks = cells.reshape(blocks, block_size)
    coord_blocks = coords.reshape(3, blocks, block_size).transpose(1, 0, 2)
    speed_blocks = speeds.reshape(3, blocks, block_size).transpose(1, 0, 2)
    rate_blocks = rates.reshape(blocks, block_size)

    def visit(force, inputs):
        cell_block, coord_block, speed_block, rate_block = inputs
        weights = basis(coord_block)
        gathered = field[:3, cell_block, :]
        fluid = jnp.sum(gathered * weights[None], axis=2)
        offset_block = fluid - speed_block
        accel = rate_block[None] * offset_block
        heat = rate_block * jnp.sum(offset_block * offset_block, axis=0)
        fresh = speed_block + step_time * accel
        sources = jnp.concatenate([accel, heat[None]], axis=0)
        force = force.at[:, cell_block, :].add(sources[:, :, None] * weights[None])
        return force, fresh

    force, fresh = lax.scan(visit, jnp.zeros(field.shape, jnp.float32), (cell_blocks, coord_blocks, speed_blocks, rate_blocks))
    new_speeds = fresh.transpose(1, 0, 2).reshape(3, total)
    return fluid_step(field, neighbours, force), new_speeds


def migrate(values, cut):
    rows = values.shape[0]
    slab = N_GY * N_GZ * BIN
    grouped = values.reshape(rows, N_GX, slab)
    doubled = jnp.concatenate([grouped, grouped], axis=2)
    moved = lax.dynamic_slice_in_dim(doubled, cut[0].astype(jnp.int32), slab, 2)
    return moved.reshape(rows, -1)


def reference(field, neighbours, cell_one, ref_one, cell_two, ref_two, velocity, rate, cut):
    middle, speeds = coupled_step(field, neighbours, cell_one, ref_one, velocity, rate)
    carried = migrate(jnp.concatenate([speeds, rate[None]], axis=0), cut)
    final, speeds_two = coupled_step(middle, neighbours, cell_two, ref_two, carried[:3], carried[3])
    return final, speeds_two
```

```python
import functools

import jax
import jax.numpy as jnp
import numpy as np
from jax import lax
from jax.experimental import pallas as pl
from jax.experimental.pallas import tpu as pltpu
from jax.sharding import PartitionSpec as P

node_points = -np.cos(np.pi * np.arange(8) / 7.0)
step_time = 0.1
viscosity = 0.002
penalty = 0.25
coupling = (-0.5, -0.5, -0.5, 0.5)

ELEMS = 64
OWNERS = 64
BIN = 2048
CAP = 64
ROWS = OWNERS * CAP // 128
CHUNK_ROWS = 4
CHUNK = 128 * CHUNK_ROWS

f32 = jnp.float32
bf16 = jnp.bfloat16
i32 = jnp.int32


def gap_table():
    differences = node_points[:, None] - node_points[None, :] + np.eye(8)
    inverse = 1.0 / differences
    return inverse * (1.0 - np.eye(8))


def laplace_table():
    differences = node_points[:, None] - node_points[None, :] + np.eye(8)
    weights = 1.0 / np.prod(differences, axis=1)
    derivative = weights[None, :] / weights[:, None] / differences
    derivative = derivative * (1.0 - np.eye(8))
    derivative = derivative - np.eye(8) * derivative.sum(axis=1)[:, None]
    second = derivative @ derivative
    identity = np.eye(8)
    operator = np.kron(np.kron(second, identity), identity)
    operator = operator + np.kron(np.kron(identity, second), identity)
    operator = operator + np.kron(np.kron(identity, identity), second)
    return operator.T


def face_table():
    selection = np.zeros((512, 384))
    for face_side in range(6):
        edge_value = 0 if face_side % 2 == 0 else 7
        for row_node in range(8):
            for col_node in range(8):
                if face_side < 2:
                    node_index = (edge_value * 8 + row_node) * 8 + col_node
                elif face_side < 4:
                    node_index = (row_node * 8 + edge_value) * 8 + col_node
                else:
                    node_index = (row_node * 8 + col_node) * 8 + edge_value
                selection[node_index, face_side * 64 + row_node * 8 + col_node] = 1.0
    return selection


def iota(shape, axis):
    return lax.broadcasted_iota(i32, shape, axis)


def split(x):
    high = x.astype(bf16)
    return high, (x - high.astype(f32)).astype(bf16)


def split_row(x):
    high = x.astype(bf16).astype(f32)
    return high, x - high


def dot(a, b):
    return jnp.dot(a, b, preferred_element_type=f32)


def dot_nt(a, b):
    return lax.dot_general(a, b, (((1,), (1,)), ((), ())), preferred_element_type=f32)


def rank_in_owner(owner):
    width = 256
    upto = jnp.where(iota((width, width), 0) <= iota((width, width), 1), 1.0, 0.0).astype(bf16)
    base = jnp.zeros((OWNERS, 1), f32)
    ranks = []
    for start in range(0, BIN, width):
        here = iota((OWNERS, width), 0) == owner[:, start : start + width]
        counts = dot(jnp.where(here, 1.0, 0.0).astype(bf16), upto)
        full = counts + base
        ranks.append(jnp.sum(jnp.where(here, full, 0.0), axis=0, keepdims=True) - 1.0)
        base = base + counts[:, width - 1 : width]
    return jnp.concatenate(ranks, axis=1)


def scatter_slots(out_ref, owner, rank, values):
    owned = jnp.where(iota((OWNERS, BIN), 0) == owner, 1.0, 0.0).astype(bf16)
    placed = iota((CAP, BIN), 0) == rank
    for first in range(0, len(values), 4):
        highs, lows = [], []
        for value in values[first : first + 4]:
            high, low = split_row(value)
            highs.append(jnp.where(placed, high, 0.0).astype(bf16))
            lows.append(jnp.where(placed, low, 0.0).astype(bf16))
        out = dot_nt(owned, jnp.concatenate(highs, axis=0)) + dot_nt(
            owned, jnp.concatenate(lows, axis=0)
        )
        out_ref[:, first // 2, :] = out[:, :128]
        out_ref[:, first // 2 + 1, :] = out[:, 128:]


def gather_slots(blocks, owner, lane_hot):
    high, low = split(jnp.concatenate(blocks, axis=0))
    rows = OWNERS * len(blocks)
    both = dot(jnp.concatenate([high, low], axis=0), lane_hot)
    total = both[:rows] + both[rows:]
    owned = iota((OWNERS, BIN), 0) == owner
    return [
        jnp.sum(jnp.where(owned, total[k * OWNERS : (k + 1) * OWNERS], 0.0), axis=0, keepdims=True)
        for k in range(len(blocks))
    ]


def send_kernel(cell_ref, coord_ref, speed_ref, rate_ref, out_ref, code_ref):
    cell = cell_ref[...]
    owner = (cell >> 6) & (OWNERS - 1)
    element = (cell & (ELEMS - 1)).astype(f32)
    rank = rank_in_owner(owner)
    code_ref[0:1, :] = owner.astype(f32) * float(CAP) + rank
    code_ref[1:2, :] = rate_ref[...]
    values = [
        element,
        speed_ref[0:1, :],
        coord_ref[0:1, :],
        speed_ref[1:2, :],
        coord_ref[1:2, :],
        speed_ref[2:3, :],
        coord_ref[2:3, :],
        rate_ref[...],
    ]
    scatter_slots(out_ref, owner, rank.astype(i32), values)


def rank_kernel(cell_ref, code_ref):
    owner = (cell_ref[...] >> 6) & (OWNERS - 1)
    code_ref[...] = owner * CAP + rank_in_owner(owner).astype(i32)


def resend_kernel(cut_ref, back_ref, moved_ref, cell_ref, code_ref, coord_ref, out_ref):
    first_code = moved_ref[0:1, :].astype(i32)
    rate = moved_ref[1:2, :]
    part = jnp.where(iota((1, BIN), 1) + cut_ref[0] >= BIN, CAP, 0)
    lane_hot = jnp.where(
        iota((128, BIN), 0) == (first_code & (CAP - 1)) + part, 1.0, 0.0
    ).astype(bf16)
    speeds = gather_slots([back_ref[:, k, :] for k in range(3)], first_code >> 6, lane_hot)
    element = (cell_ref[...] & (ELEMS - 1)).astype(f32)
    code = code_ref[...]
    values = [
        element,
        speeds[0],
        coord_ref[0:1, :],
        speeds[1],
        coord_ref[1:2, :],
        speeds[2],
        coord_ref[2:3, :],
        rate,
    ]
    scatter_slots(out_ref, code >> 6, code & (CAP - 1), values)


def final_kernel(back_ref, code_ref, out_ref):
    code = code_ref[...]
    lane_hot = jnp.where(
        (iota((128, BIN), 0) & (CAP - 1)) == (code & (CAP - 1)), 1.0, 0.0
    ).astype(bf16)
    left = iota((OWNERS, 128), 1) < 64
    pair, last = back_ref[:, 0, :], back_ref[:, 1, :]
    blocks = [jnp.where(left, pair, 0.0), jnp.where(left, 0.0, pair), jnp.where(left, last, 0.0)]
    speeds = gather_slots(blocks, code >> 6, lane_hot)
    for k in range(3):
        out_ref[k : k + 1, :] = speeds[k]


def lagrange(x):
    inverse = gap_table()
    row = iota((8, 1), 0)
    result = None
    for m in range(8):
        column = jnp.zeros((8, 1), f32)
        for a in range(8):
            column = jnp.where(row == a, float(inverse[a, m]), column)
        factor = (x - float(node_points[m])) * column + jnp.where(row == m, 1.0, 0.0)
        result = factor if result is None else result * factor
    return result


def basis(coords):
    first, second, third = [lagrange(x) for x in coords]
    pieces = []
    for a in range(8):
        pair = first[a : a + 1, :] * second
        for b in range(8):
            pieces.append(pair[b : b + 1, :] * third)
    return jnp.concatenate(pieces, axis=0)


def along(rows, k):
    return jnp.concatenate([rows[i, k : k + 1, :] for i in range(CHUNK_ROWS)], axis=1)


def unfold(incoming_ref, even_ref, odd_ref):
    low, high = incoming_ref[0 : ROWS], incoming_ref[ROWS : 2 * ROWS]
    left = iota(low.shape, 2) < 64
    even_ref[...] = jnp.where(left, low, pltpu.roll(high, 64, 2))
    odd_ref[...] = jnp.where(left, pltpu.roll(low, 64, 2), high)


def interpolate_kernel(shift, incoming_ref, state_ref, back_ref, source_ref, even_ref, odd_ref, fresh_ref, state_scr):
    unfold(incoming_ref, even_ref, odd_ref)
    high, low = split(state_ref[0:3].reshape(3 * ELEMS, 512))
    state_scr[0 : 3 * ELEMS] = high
    state_scr[3 * ELEMS :] = low

    def visit(index, carry):
        start = index * CHUNK_ROWS
        even = even_ref[pl.ds(start, CHUNK_ROWS)]
        odd = odd_ref[pl.ds(start, CHUNK_ROWS)]
        weight_high, weight_low = split(basis([along(even, k) for k in (1, 2, 3)]))
        wide = dot(state_scr[...], weight_high)
        values = wide[: 3 * ELEMS] + wide[3 * ELEMS :]
        values = values + dot(state_scr[0 : 3 * ELEMS], weight_low)
        here = iota((ELEMS, CHUNK), 0) == along(even, 0).astype(i32)
        rates = along(odd, 3)
        squares = None
        fresh, sources = [], []
        for k in range(3):
            picked = jnp.where(here, values[k * ELEMS : (k + 1) * ELEMS], 0.0)
            speed = along(odd, k)
            offset = jnp.sum(picked, axis=0, keepdims=True) - speed
            accel = rates * offset
            squares = offset * offset if squares is None else squares + offset * offset
            sources.append(accel)
            fresh.append(speed + step_time * accel)
        sources.append(rates * squares)
        for i in range(CHUNK_ROWS):
            lanes = slice(i * 128, (i + 1) * 128)
            for k in range(4):
                source_ref[start + i, k : k + 1, :] = sources[k][:, lanes]
            for k in range(3):
                fresh_ref[start + i, k : k + 1, :] = fresh[k][:, lanes]
        return carry

    fresh_ref[:, 3:4, :] = jnp.zeros((ROWS + 1, 1, 128), f32)
    lax.fori_loop(0, ROWS // CHUNK_ROWS, visit, 0)
    fresh = fresh_ref[0:ROWS]
    if shift:
        fresh_ref[ROWS] = pltpu.roll(fresh_ref[0], 64, 1)
        after = fresh_ref[1 : ROWS + 1]
        left = iota(fresh.shape, 2) < 64
        back_ref[0:ROWS] = jnp.where(left, fresh, pltpu.roll(after, 64, 2))
        back_ref[ROWS : 2 * ROWS] = jnp.where(left, pltpu.roll(fresh, 64, 2), after)
    else:
        turned = pltpu.roll(fresh, 64, 2)
        left = iota((ROWS, 1, 128), 2) < 64
        back_ref[0:ROWS, 0:1, :] = jnp.where(left, fresh[:, 0:1, :], turned[:, 1:2, :])
        back_ref[0:ROWS, 1:2, :] = fresh[:, 2:3, :]
        back_ref[ROWS : 2 * ROWS, 0:1, :] = jnp.where(left, turned[:, 0:1, :], fresh[:, 1:2, :])
        back_ref[ROWS : 2 * ROWS, 1:2, :] = turned[:, 2:3, :]


def force_kernel(incoming_ref, source_ref, base_ref, out_ref, even_ref, odd_ref, total_ref):
    unfold(incoming_ref, even_ref, odd_ref)
    total_ref[...] = jnp.zeros_like(total_ref)

    def visit(index, carry):
        start = index * CHUNK_ROWS
        even = even_ref[pl.ds(start, CHUNK_ROWS)]
        rows = source_ref[pl.ds(start, CHUNK_ROWS)]
        weight_high, weight_low = split(basis([along(even, k) for k in (1, 2, 3)]))
        here = iota((ELEMS, CHUNK), 0) == along(even, 0).astype(i32)
        highs, lows = [], []
        for k in range(4):
            high, low = split_row(along(rows, k))
            highs.append(jnp.where(here, high, 0.0).astype(bf16))
            lows.append(jnp.where(here, low, 0.0).astype(bf16))
        high = jnp.concatenate(highs, axis=0)
        wide = dot_nt(jnp.concatenate([high] + lows, axis=0), weight_high)
        total_ref[...] += wide[: 4 * ELEMS] + wide[4 * ELEMS :] + dot_nt(high, weight_low)
        return carry

    lax.fori_loop(0, ROWS // CHUNK_ROWS, visit, 0)
    for k in range(4):
        out_ref[k] = base_ref[k] + coupling[k] * total_ref[k * ELEMS : (k + 1) * ELEMS]


def faces_kernel(device_ref, state_ref, near_ref, near_t_ref, select_ref, faces_ref, *send_refs):
    high, low = split(state_ref[...].reshape(4 * ELEMS, 512))
    picked = dot(jnp.concatenate([high, low], axis=0), select_ref[...])
    picked = picked[: 4 * ELEMS] + picked[4 * ELEMS :]
    left = iota((ELEMS, 128), 1) < 64
    device = device_ref[0]
    for pair in range(3):
        tiles = [picked[k * ELEMS : (k + 1) * ELEMS, pair * 128 : (pair + 1) * 128] for k in range(4)]
        turned = [pltpu.roll(tile, 64, 1) for tile in tiles]
        lower = [jnp.where(left, tiles[k], turned[k + 1]) for k in (0, 2)]
        upper = [jnp.where(left, turned[k], tiles[k + 1]) for k in (0, 2)]
        for side, parts in ((2 * pair, lower), (2 * pair + 1, upper)):
            face = jnp.concatenate(parts, axis=1)
            faces_ref[side] = face
            outside = (near_ref[:, side : side + 1] >> 6) != device
            outside_t = (near_t_ref[side : side + 1, :] >> 6) != device
            before = (iota((ELEMS, ELEMS), 0) < iota((ELEMS, ELEMS), 1)) & outside
            rank = jnp.sum(jnp.where(before, 1.0, 0.0), axis=0, keepdims=True)
            chosen = (iota((16, ELEMS), 0).astype(f32) == rank) & outside_t
            chosen = jnp.where(chosen, 1.0, 0.0).astype(bf16)
            face_high, face_low = split(face)
            send_refs[side][...] = dot(chosen, face_high) + dot(chosen, face_low)


def fluid_kernel(device_ref, state_ref, faces_ref, near_ref, near_t_ref, select_t_ref, lap_high_ref, lap_low_ref, keep_ref, *refs):
    halo_refs, out_ref = refs[:6], refs[6]
    device = device_ref[0]
    partners = []
    for side in range(6):
        target = near_ref[:, side : side + 1]
        target_t = near_t_ref[side : side + 1, :]
        local = (target >> 6) == device
        remote = (target >= 0) & ((target >> 6) != device)
        remote_t = (target_t >= 0) & ((target_t >> 6) != device)
        slot = target & (ELEMS - 1)
        own = ((iota((ELEMS, 2 * ELEMS), 1) & (ELEMS - 1)) == slot) & local
        key = jnp.where(remote, slot, ELEMS)
        key_t = jnp.where(remote_t, target_t & (ELEMS - 1), ELEMS)
        rank = jnp.sum(jnp.where(key_t < key, 1.0, 0.0), axis=1, keepdims=True)
        far = ((iota((ELEMS, 32), 1) & 15).astype(f32) == rank) & remote
        face = jnp.concatenate(split(faces_ref[side ^ 1]), axis=0)
        halo = jnp.concatenate(split(halo_refs[side][...]), axis=0)
        partners.append(
            dot(jnp.where(own, 1.0, 0.0).astype(bf16), face)
            + dot(jnp.where(far, 1.0, 0.0).astype(bf16), halo)
        )
    left = iota((ELEMS, 128), 1) < 64
    turned = [[pltpu.roll(p[:, h * 128 : (h + 1) * 128], 64, 1) for h in range(2)] for p in partners]
    joined = []
    for k in range(4):
        h = k // 2
        row = []
        for pair in range(3):
            lower, upper = partners[2 * pair], partners[2 * pair + 1]
            lanes = slice(h * 128, (h + 1) * 128)
            if k % 2 == 0:
                row.append(jnp.where(left, lower[:, lanes], turned[2 * pair + 1][h]))
            else:
                row.append(jnp.where(left, turned[2 * pair][h], upper[:, lanes]))
        joined.append(jnp.concatenate(row, axis=1))
    high, low = split(jnp.concatenate(joined, axis=0))
    spread = dot(jnp.concatenate([high, low], axis=0), select_t_ref[...])
    spread = spread[: 4 * ELEMS] + spread[4 * ELEMS :]
    state = state_ref[...].reshape(4 * ELEMS, 512)
    high, low = split(state)
    wide = dot(jnp.concatenate([high, low], axis=0), lap_high_ref[...])
    laplace = wide[: 4 * ELEMS] + wide[4 * ELEMS :] + dot(high, lap_low_ref[...])
    result = state * keep_ref[...] + viscosity * laplace + penalty * spread
    out_ref[...] = result.reshape(4, ELEMS, 512)


def call(kernel, shapes, scratch=(), scalars=0, name=None):
    vmem = pl.BlockSpec(memory_space=pltpu.VMEM)
    smem = pl.BlockSpec(memory_space=pltpu.SMEM)

    def run(*args):
        return pl.pallas_call(
            kernel,
            out_shape=shapes,
            in_specs=[smem] * scalars + [vmem] * (len(args) - scalars),
            out_specs=jax.tree.map(lambda _: vmem, shapes),
            scratch_shapes=list(scratch),
            name=name,
        )(*args)

    return run


def shape(*dims, dtype=f32):
    return jax.ShapeDtypeStruct(dims, dtype)


def local(field, neighbours, cell_one, ref_one, cell_two, ref_two, velocity, rate, cut):
    device = lax.axis_index(("gx", "gy", "gz")).astype(i32).reshape(1)
    near_t = neighbours.T
    select = jnp.asarray(face_table(), bf16)
    select_t = jnp.asarray(face_table().T, bf16)
    lap = laplace_table()
    lap_high = jnp.asarray(lap, bf16)
    lap_low = jnp.asarray(lap - np.asarray(np.asarray(lap, bf16), np.float64), bf16)
    keep = jnp.asarray(1.0 - penalty * face_table().sum(axis=1), f32)[None]
    row_one, row_two = cell_one[None], cell_two[None]
    slots = shape(OWNERS, 4, 128)

    def exchange(block):
        return lax.all_to_all(block, ("gy", "gz"), split_axis=0, concat_axis=0, tiled=True)

    def neighbour_faces(sends):
        arrived = [None] * 6
        for axis_index, axis in enumerate(("gx", "gy", "gz")):
            count = lax.axis_size(axis)
            span = count if axis == "gz" else count - 1
            up = [(i, (i + 1) % count) for i in range(span)]
            arrived[2 * axis_index] = lax.ppermute(sends[2 * axis_index + 1], axis, up)
            arrived[2 * axis_index + 1] = lax.ppermute(
                sends[2 * axis_index], axis, [(b, a) for a, b in up]
            )
        return arrived

    def faces(state):
        face_shapes = [shape(6, ELEMS, 256)] + [shape(16, 256)] * 6
        out = call(faces_kernel, face_shapes, scalars=1, name="faces")(
            device, state, neighbours, near_t, select
        )
        return out[0], neighbour_faces(out[1:])

    def fluid(state, own, arrived):
        return call(fluid_kernel, shape(4, ELEMS, 512), scalars=1, name="fluid")(
            device, state, own, neighbours, near_t, select_t, lap_high, lap_low, keep, *arrived
        )

    pair_scratch = [pltpu.VMEM((ROWS, 4, 128), f32), pltpu.VMEM((ROWS, 4, 128), f32)]

    def interpolate(incoming, state, shift):
        back = slots if shift else shape(OWNERS, 2, 128)
        return call(
            functools.partial(interpolate_kernel, shift),
            [back, shape(ROWS, 4, 128)],
            scratch=pair_scratch
            + [pltpu.VMEM((ROWS + 1, 4, 128), f32), pltpu.VMEM((6 * ELEMS, 512), bf16)],
            name="interpolate",
        )(incoming, state)

    def add_force(incoming, sources, base):
        return call(
            force_kernel,
            shape(4, ELEMS, 512),
            scratch=pair_scratch + [pltpu.VMEM((4 * ELEMS, 512), f32)],
            name="force",
        )(incoming, sources, base)

    outgoing, code_rate = call(send_kernel, [slots, shape(2, BIN)], name="send")(
        row_one, ref_one, velocity, rate[None]
    )
    incoming = exchange(outgoing)
    owners = lax.axis_size("gy") * lax.axis_size("gz")
    following = lax.ppermute(
        code_rate, ("gy", "gz"), [((i + 1) % owners, i) for i in range(owners)]
    )
    moved = lax.dynamic_slice_in_dim(
        jnp.concatenate([code_rate, following], axis=1), cut[0], BIN, 1
    )
    code_two = call(rank_kernel, shape(1, BIN, dtype=i32), name="rank")(row_two)
    base = fluid(field, *faces(field))

    back, sources = interpolate(incoming, field, True)
    returned = exchange(back)
    middle = add_force(incoming, sources, base)
    outgoing = call(resend_kernel, slots, scalars=1, name="resend")(
        cut, returned, moved, row_two, code_two, ref_two
    )
    incoming = exchange(outgoing)
    base = fluid(middle, *faces(middle))
    back, sources = interpolate(incoming, middle, False)
    returned = exchange(back)
    final_state = add_force(incoming, sources, base)
    final_speeds = call(final_kernel, shape(3, BIN), name="final")(returned, code_two)
    return (final_state, final_speeds)


def solution(mesh):
    in_specs = (
        P(None, ("gx", "gy", "gz"), None),
        P(("gx", "gy", "gz"), None),
        P(("gx", "gy", "gz")),
        P(None, ("gx", "gy", "gz")),
        P(("gx", "gy", "gz")),
        P(None, ("gx", "gy", "gz")),
        P(None, ("gx", "gy", "gz")),
        P(("gx", "gy", "gz")),
        P(),
    )
    out_specs = (P(None, ("gx", "gy", "gz"), None), P(None, ("gx", "gy", "gz")))
    return jax.shard_map(local, mesh=mesh, in_specs=in_specs, out_specs=out_specs, check_vma=False)
```

```python
import functools

import jax
import jax.numpy as jnp
import numpy as np
from jax import lax
from jax.experimental import pallas as pl
from jax.experimental.pallas import tpu as pltpu
from jax.sharding import PartitionSpec as P

node_points = -np.cos(np.pi * np.arange(8) / 7.0)
step_time = 0.1
viscosity = 0.002
penalty = 0.25
loading = 0.5
heating = 0.5

ELEMS = 64
OWNERS = 64
BIN = 2048
CAP = 64
ROWS = OWNERS * CAP // 128
CHUNK_ROWS = 4
CHUNK = 128 * CHUNK_ROWS
BODY = 2

f32 = jnp.float32
bf16 = jnp.bfloat16
i32 = jnp.int32


def laplace_table():
    differences = node_points[:, None] - node_points[None, :] + np.eye(8)
    weights = 1.0 / np.prod(differences, axis=1)
    derivative = weights[None, :] / weights[:, None] / differences
    derivative = derivative * (1.0 - np.eye(8))
    derivative = derivative - np.eye(8) * derivative.sum(axis=1)[:, None]
    second = derivative @ derivative
    identity = np.eye(8)
    operator = np.kron(np.kron(second, identity), identity)
    operator = operator + np.kron(np.kron(identity, second), identity)
    operator = operator + np.kron(np.kron(identity, identity), second)
    return operator.T


def face_table():
    selection = np.zeros((512, 384))
    for face_side in range(6):
        edge_value = 0 if face_side % 2 == 0 else 7
        for row_node in range(8):
            for col_node in range(8):
                if face_side < 2:
                    node_index = (edge_value * 8 + row_node) * 8 + col_node
                elif face_side < 4:
                    node_index = (row_node * 8 + edge_value) * 8 + col_node
                else:
                    node_index = (row_node * 8 + col_node) * 8 + edge_value
                selection[node_index, face_side * 64 + row_node * 8 + col_node] = 1.0
    return selection


def iota(shape, axis):
    return lax.broadcasted_iota(i32, shape, axis)


def split(x):
    high = x.astype(bf16)
    return high, (x - high.astype(f32)).astype(bf16)


def split_row(x):
    high = x.astype(bf16).astype(f32)
    return high, x - high


def dot(a, b):
    return jnp.dot(a, b, preferred_element_type=f32)


def dot_nt(a, b):
    return lax.dot_general(a, b, (((1,), (1,)), ((), ())), preferred_element_type=f32)


def rank_in_owner(owner):
    width = 256
    upto = jnp.where(iota((width, width), 0) <= iota((width, width), 1), 1.0, 0.0).astype(bf16)
    table = jnp.concatenate([upto, jnp.ones((width, width), bf16)], axis=0)
    before = jnp.zeros((OWNERS, width), f32)
    ranks = []
    for start in range(0, BIN, width):
        here = iota((OWNERS, width), 0) == owner[:, start : start + width]
        marks = jnp.where(here, 1.0, 0.0)
        counts = dot(jnp.concatenate([marks, before], axis=1).astype(bf16), table)
        ranks.append(jnp.sum(jnp.where(here, counts, 0.0), axis=0, keepdims=True) - 1.0)
        before = before + marks
    return jnp.concatenate(ranks, axis=1)


def thick(row, rows):
    sixteen = jnp.broadcast_to(row, (16, row.shape[1])).astype(bf16)
    return jnp.concatenate([sixteen] * (rows // 16), axis=0)


def one_hot(index, rows):
    return jnp.where(iota((rows, index.shape[1]), 0) == index, 1.0, 0.0).astype(bf16)


def scatter_slots(out_ref, owner, rank, values):
    owned = one_hot(owner, OWNERS)
    placed = one_hot(rank, CAP)
    for first in range(0, len(values), 4):
        highs, lows = [], []
        for value in values[first : first + 4]:
            high, low = split_row(value)
            highs.append(placed * thick(high, CAP))
            lows.append(placed * thick(low, CAP))
        out = dot_nt(owned, jnp.concatenate(highs, axis=0)) + dot_nt(
            owned, jnp.concatenate(lows, axis=0)
        )
        out_ref[:, first // 2, :] = out[:, :128]
        out_ref[:, first // 2 + 1, :] = out[:, 128:]


def gather_slots(blocks, owner, lane_hot):
    high, low = split(jnp.concatenate(blocks, axis=0))
    total = dot(jnp.concatenate([high, low], axis=1), jnp.concatenate([lane_hot] * 2, axis=0))
    owned = iota((OWNERS, BIN), 0) == owner
    return [
        jnp.sum(jnp.where(owned, total[k * OWNERS : (k + 1) * OWNERS], 0.0), axis=0, keepdims=True)
        for k in range(len(blocks))
    ]


def send_kernel(cell_ref, coord_ref, speed_ref, rate_ref, out_ref, code_ref):
    cell = cell_ref[...]
    owner = (cell >> 6) & (OWNERS - 1)
    element = (cell & (ELEMS - 1)).astype(f32)
    rank = rank_in_owner(owner)
    code_ref[0:1, :] = owner.astype(f32) * float(CAP) + rank
    code_ref[1:2, :] = rate_ref[...]
    values = [
        element,
        speed_ref[0:1, :],
        coord_ref[0:1, :],
        speed_ref[1:2, :],
        coord_ref[1:2, :],
        speed_ref[2:3, :],
        coord_ref[2:3, :],
        rate_ref[...],
    ]
    scatter_slots(out_ref, owner, rank.astype(i32), values)


def resend_kernel(cut_ref, back_ref, moved_ref, cell_ref, code_ref, coord_ref, out_ref):
    first_code = moved_ref[0:1, :].astype(i32)
    rate = moved_ref[1:2, :]
    part = jnp.where(iota((1, BIN), 1) + cut_ref[0] >= BIN, CAP, 0)
    lane_hot = one_hot((first_code & (CAP - 1)) + part, 128)
    speeds = gather_slots([back_ref[:, k, :] for k in range(3)], first_code >> 6, lane_hot)
    element = (cell_ref[...] & (ELEMS - 1)).astype(f32)
    code = code_ref[...]
    values = [
        element,
        speeds[0],
        coord_ref[0:1, :],
        speeds[1],
        coord_ref[1:2, :],
        speeds[2],
        coord_ref[2:3, :],
        rate,
    ]
    scatter_slots(out_ref, code >> 6, code & (CAP - 1), values)


def final_kernel(back_ref, code_ref, out_ref):
    code = code_ref[...]
    lane_hot = jnp.concatenate([one_hot(code & (CAP - 1), CAP)] * 2, axis=0)
    left = iota((OWNERS, 128), 1) < 64
    pair, last = back_ref[:, 0, :], back_ref[:, 1, :]
    blocks = [jnp.where(left, pair, 0.0), jnp.where(left, 0.0, pair), jnp.where(left, last, 0.0)]
    speeds = gather_slots(blocks, code >> 6, lane_hot)
    for k in range(3):
        out_ref[k : k + 1, :] = speeds[k]


def column(values):
    row = iota((8, 1), 0)
    result = jnp.zeros((8, 1), f32)
    for index, value in enumerate(values):
        result = jnp.where(row == index, float(value), result)
    return result


def lagrange(x):
    gaps = node_points[:, None] - node_points[None, :] + np.eye(8)
    one = pltpu.roll(x - column(node_points), 1, 0)
    two = one * pltpu.roll(one, 1, 0)
    four = two * pltpu.roll(two, 2, 0)
    last = pltpu.roll(one, 6, 0) * column(1.0 / np.prod(gaps, axis=1))
    return four * pltpu.roll(two, 4, 0) * last


def basis(coords, pair_ref, weight_ref):
    first, second, third = [lagrange(x) for x in coords]
    for a in range(8):
        pair_ref[8 * a : 8 * a + 8, :] = first[a : a + 1, :] * second
    for i in range(32):
        piece = jnp.concatenate(
            [pair_ref[2 * i + h : 2 * i + h + 1, :] * third for h in range(2)], axis=0
        )
        weight_ref[16 * i : 16 * i + 16, :], weight_ref[512 + 16 * i : 528 + 16 * i, :] = split(piece)


def along(rows, k):
    return jnp.concatenate([rows[i, k : k + 1, :] for i in range(CHUNK_ROWS)], axis=1)


def particle_kernel(shift, incoming_ref, state_ref, back_ref, force_ref, even_ref, odd_ref, fresh_ref, state_scr, pair_refs, weight_refs, source_refs, total_ref):
    low, high = incoming_ref[0:ROWS], incoming_ref[ROWS : 2 * ROWS]
    left = iota(low.shape, 2) < 64
    even_ref[...] = jnp.where(left, low, pltpu.roll(high, 64, 2))
    odd_ref[...] = jnp.where(left, pltpu.roll(low, 64, 2), high)
    high, low = split(state_ref[0:3].reshape(3 * ELEMS, 512))
    state_scr[0 : 3 * ELEMS] = high
    state_scr[3 * ELEMS :] = low
    fresh_ref[:, 3:4, :] = jnp.zeros((ROWS + 1, 1, 128), f32)

    total_ref[...] = jnp.zeros_like(total_ref)

    def one(start, weight_ref, source_ref, pair_ref):
        even = even_ref[pl.ds(start, CHUNK_ROWS)]
        odd = odd_ref[pl.ds(start, CHUNK_ROWS)]
        basis([along(even, k) for k in (1, 2, 3)], pair_ref, weight_ref)
        wide = dot(state_scr[...], weight_ref[0:512])
        rest = dot(state_scr[0 : 3 * ELEMS], weight_ref[512:1024])
        element = along(even, 0).astype(i32)
        here = iota((ELEMS, CHUNK), 0) == element
        rates = along(odd, 3)
        squares = None
        fresh, sources = [], []
        for k in range(3):
            rows = slice(k * ELEMS, (k + 1) * ELEMS)
            lower = slice((k + 3) * ELEMS, (k + 4) * ELEMS)
            picked = jnp.where(here, wide[rows] + wide[lower] + rest[rows], 0.0)
            speed = along(odd, k)
            offset = jnp.sum(picked, axis=0, keepdims=True) - speed
            accel = rates * offset
            squares = offset * offset if squares is None else squares + offset * offset
            sources.append(accel)
            fresh.append(speed + step_time * accel)
        sources.append(rates * squares)
        for i in range(CHUNK_ROWS):
            for k in range(3):
                fresh_ref[start + i, k : k + 1, :] = fresh[k][:, i * 128 : (i + 1) * 128]
        hot = one_hot(element, ELEMS)
        for k in range(4):
            high, low = split_row(sources[k])
            source_ref[0, k * ELEMS : (k + 1) * ELEMS] = hot * thick(high, ELEMS)
            source_ref[1, k * ELEMS : (k + 1) * ELEMS] = hot * thick(low, ELEMS)

    def push(weight_ref, source_ref):
        wide = dot_nt(weight_ref[...], source_ref[0])
        total_ref[...] += wide[:512] + wide[512:] + dot_nt(weight_ref[0:512], source_ref[1])

    def visit(index, carry):
        for h in range(BODY):
            one((index * BODY + h) * CHUNK_ROWS, weight_refs.at[h], source_refs.at[h], pair_refs.at[h])
        for h in range(BODY):
            push(weight_refs.at[h], source_refs.at[h])
        return carry

    lax.fori_loop(0, ROWS // CHUNK_ROWS // BODY, visit, 0)
    fresh = fresh_ref[0:ROWS]
    if shift:
        fresh_ref[ROWS] = pltpu.roll(fresh_ref[0], 64, 1)
        after = fresh_ref[1 : ROWS + 1]
        left = iota(fresh.shape, 2) < 64
        back_ref[0:ROWS] = jnp.where(left, fresh, pltpu.roll(after, 64, 2))
        back_ref[ROWS : 2 * ROWS] = jnp.where(left, pltpu.roll(fresh, 64, 2), after)
    else:
        turned = pltpu.roll(fresh, 64, 2)
        left = iota((ROWS, 1, 128), 2) < 64
        back_ref[0:ROWS, 0:1, :] = jnp.where(left, fresh[:, 0:1, :], turned[:, 1:2, :])
        back_ref[0:ROWS, 1:2, :] = fresh[:, 2:3, :]
        back_ref[ROWS : 2 * ROWS, 0:1, :] = jnp.where(left, turned[:, 0:1, :], fresh[:, 1:2, :])
        back_ref[ROWS : 2 * ROWS, 1:2, :] = turned[:, 2:3, :]
    force_ref[...] = total_ref[...].T


def pick_faces(state, select_ref, chosen_ref, faces_ref, send_refs):
    high, low = split(state)
    picked = dot(jnp.concatenate([high, low], axis=0), select_ref[...])
    picked = picked[: 4 * ELEMS] + picked[4 * ELEMS :]
    left = iota((ELEMS, 128), 1) < 64
    for pair in range(3):
        tiles = [picked[k * ELEMS : (k + 1) * ELEMS, pair * 128 : (pair + 1) * 128] for k in range(4)]
        turned = [pltpu.roll(tile, 64, 1) for tile in tiles]
        lower = [jnp.where(left, tiles[k], turned[k + 1]) for k in (0, 2)]
        upper = [jnp.where(left, turned[k], tiles[k + 1]) for k in (0, 2)]
        for side, parts in ((2 * pair, lower), (2 * pair + 1, upper)):
            face = jnp.concatenate(parts, axis=1)
            faces_ref[side] = face
            face_high, face_low = split(face)
            send_refs[side][...] = dot(chosen_ref[side], face_high) + dot(chosen_ref[side], face_low)


def links_kernel(device_ref, state_ref, near_t_ref, cell_ref, select_ref, code_ref, own_ref, far_ref, chosen_ref, faces_ref, *send_refs):
    device = device_ref[0]
    near_t = near_t_ref[...].astype(f32)
    near = jnp.concatenate([near_t, near_t[0:2]], axis=0).T.astype(i32)
    for side in range(6):
        target = near[:, side : side + 1]
        target_t = near_t_ref[side : side + 1, :]
        outside = (target >> 6) != device
        outside_t = (target_t >> 6) != device
        remote = (target >= 0) & outside
        remote_t = (target_t >= 0) & outside_t
        slot = jnp.where(outside, -1, target & (ELEMS - 1))
        own = (iota((ELEMS, 2 * ELEMS), 1) & (ELEMS - 1)) == slot
        own_ref[side] = jnp.where(own, 1.0, 0.0).astype(bf16)
        key = jnp.where(remote, target & (ELEMS - 1), ELEMS)
        key_t = jnp.where(remote_t, target_t & (ELEMS - 1), ELEMS)
        rank = jnp.sum(jnp.where(key_t < key, 1.0, 0.0), axis=1, keepdims=True)
        rank = jnp.where(remote, rank, -1.0)
        far = (iota((ELEMS, 32), 1) & 15).astype(f32) == rank
        far_ref[side] = jnp.where(far, 1.0, 0.0).astype(bf16)
        before = (iota((ELEMS, ELEMS), 0) < iota((ELEMS, ELEMS), 1)) & outside
        rank = jnp.sum(jnp.where(before, 1.0, 0.0), axis=0, keepdims=True)
        rank = jnp.where(outside_t, rank, -1.0)
        chosen = iota((16, ELEMS), 0).astype(f32) == rank
        chosen_ref[side] = jnp.where(chosen, 1.0, 0.0).astype(bf16)
    pick_faces(state_ref[...].reshape(4 * ELEMS, 512), select_ref, chosen_ref, faces_ref, send_refs)
    owner = (cell_ref[...] >> 6) & (OWNERS - 1)
    code_ref[...] = owner * CAP + rank_in_owner(owner).astype(i32)


def fluid_kernel(again, state_ref, force_ref, own_ref, far_ref, select_t_ref, lap_high_ref, lap_low_ref, keep_ref, faces_ref, *refs):
    halo_refs, refs = refs[:6], refs[6:]
    if again:
        select_ref, chosen_ref, out_ref, next_ref = refs[:4]
        send_refs = refs[4:]
    else:
        (out_ref,) = refs
    partners = []
    for side in range(6):
        face = jnp.concatenate(split(faces_ref[side ^ 1]), axis=0)
        halo = jnp.concatenate(split(halo_refs[side][...]), axis=0)
        partners.append(dot(own_ref[side], face) + dot(far_ref[side], halo))
    left = iota((ELEMS, 128), 1) < 64
    turned = [[pltpu.roll(p[:, h * 128 : (h + 1) * 128], 64, 1) for h in range(2)] for p in partners]
    joined = []
    for k in range(4):
        h = k // 2
        row = []
        for pair in range(3):
            lower, upper = partners[2 * pair], partners[2 * pair + 1]
            lanes = slice(h * 128, (h + 1) * 128)
            if k % 2 == 0:
                row.append(jnp.where(left, lower[:, lanes], turned[2 * pair + 1][h]))
            else:
                row.append(jnp.where(left, turned[2 * pair][h], upper[:, lanes]))
        joined.append(jnp.concatenate(row, axis=1))
    high, low = split(jnp.concatenate(joined, axis=0))
    spread = dot(jnp.concatenate([high, low], axis=0), select_t_ref[...])
    spread = spread[: 4 * ELEMS] + spread[4 * ELEMS :]
    state = state_ref[...].reshape(4 * ELEMS, 512)
    high, low = split(state)
    wide = dot(jnp.concatenate([high, low], axis=0), lap_high_ref[...])
    laplace = wide[: 4 * ELEMS] + wide[4 * ELEMS :] + dot(high, lap_low_ref[...])
    result = state * keep_ref[...] + viscosity * laplace + penalty * spread
    row = iota((4 * ELEMS, 1), 0)
    result = result + jnp.where(row < 3 * ELEMS, -loading, heating) * force_ref[...]
    out_ref[...] = result.reshape(4, ELEMS, 512)
    if again:
        pick_faces(result, select_ref, chosen_ref, next_ref, send_refs)


def call(kernel, shapes, scratch=(), scalars=0, name=None):
    vmem = pl.BlockSpec(memory_space=pltpu.VMEM)
    smem = pl.BlockSpec(memory_space=pltpu.SMEM)

    def run(*args):
        return pl.pallas_call(
            kernel,
            out_shape=shapes,
            in_specs=[smem] * scalars + [vmem] * (len(args) - scalars),
            out_specs=jax.tree.map(lambda _: vmem, shapes),
            scratch_shapes=list(scratch),
            name=name,
        )(*args)

    return run


def shape(*dims, dtype=f32):
    return jax.ShapeDtypeStruct(dims, dtype)


def local(field, neighbours, cell_one, ref_one, cell_two, ref_two, velocity, rate, cut):
    device = lax.axis_index(("gx", "gy", "gz")).astype(i32).reshape(1)
    near_t = neighbours.T
    select = jnp.asarray(face_table(), bf16)
    select_t = jnp.asarray(face_table().T, bf16)
    lap = laplace_table()
    lap_high = jnp.asarray(lap, bf16)
    lap_low = jnp.asarray(lap - np.asarray(np.asarray(lap, bf16), np.float64), bf16)
    keep = jnp.asarray(1.0 - penalty * face_table().sum(axis=1), f32)[None]
    row_one, row_two = cell_one[None], cell_two[None]
    slots = shape(OWNERS, 4, 128)

    def exchange(block):
        return lax.all_to_all(block, ("gy", "gz"), split_axis=0, concat_axis=0, tiled=True)

    def neighbour_faces(sends):
        arrived = [None] * 6
        for axis_index, axis in enumerate(("gx", "gy", "gz")):
            count = lax.axis_size(axis)
            span = count if axis == "gz" else count - 1
            up = [(i, (i + 1) % count) for i in range(span)]
            arrived[2 * axis_index] = lax.ppermute(sends[2 * axis_index + 1], axis, up)
            arrived[2 * axis_index + 1] = lax.ppermute(
                sends[2 * axis_index], axis, [(b, a) for a, b in up]
            )
        return arrived

    face_shapes = [shape(6, ELEMS, 256)] + [shape(16, 256)] * 6

    def particles(incoming, state, shift):
        back = slots if shift else shape(OWNERS, 2, 128)
        return call(
            functools.partial(particle_kernel, shift),
            [back, shape(4 * ELEMS, 512)],
            scratch=[
                pltpu.VMEM((ROWS, 4, 128), f32),
                pltpu.VMEM((ROWS, 4, 128), f32),
                pltpu.VMEM((ROWS + 1, 4, 128), f32),
                pltpu.VMEM((6 * ELEMS, 512), bf16),
                pltpu.VMEM((BODY, 64, CHUNK), f32),
                pltpu.VMEM((BODY, 1024, CHUNK), bf16),
                pltpu.VMEM((BODY, 2, 4 * ELEMS, CHUNK), bf16),
                pltpu.VMEM((512, 4 * ELEMS), f32),
            ],
            name="particles",
        )(incoming, state)

    outgoing, code_rate = call(send_kernel, [slots, shape(2, BIN)], name="send")(
        row_one, ref_one, velocity, rate[None]
    )
    incoming = exchange(outgoing)
    owners = lax.axis_size("gy") * lax.axis_size("gz")
    following = lax.ppermute(
        code_rate, ("gy", "gz"), [((i + 1) % owners, i) for i in range(owners)]
    )
    moved = lax.dynamic_slice_in_dim(
        jnp.concatenate([code_rate, following], axis=1), cut[0], BIN, 1
    )
    hots = [
        shape(6, ELEMS, 2 * ELEMS, dtype=bf16),
        shape(6, ELEMS, 32, dtype=bf16),
        shape(6, 16, ELEMS, dtype=bf16),
    ]
    code_two, own, far, chosen, faces, *sends = call(
        links_kernel, [shape(1, BIN, dtype=i32)] + hots + face_shapes, scalars=1, name="links"
    )(device, field, near_t, row_two, select)
    arrived = neighbour_faces(sends)
    tables = (own, far, select_t, lap_high, lap_low, keep)

    incoming, moved, *arrived = lax.optimization_barrier((incoming, moved, *arrived))
    back, force = particles(incoming, field, True)
    returned = exchange(back)
    middle, faces, *sends = call(
        functools.partial(fluid_kernel, True), [shape(4, ELEMS, 512)] + face_shapes, name="fluid"
    )(field, force, *tables, faces, *arrived, select, chosen)
    returned, middle, *sends = lax.optimization_barrier((returned, middle, *sends))
    arrived = neighbour_faces(sends)
    outgoing = call(resend_kernel, slots, scalars=1, name="resend")(
        cut, returned, moved, row_two, code_two, ref_two
    )
    incoming = exchange(outgoing)
    incoming, *arrived = lax.optimization_barrier((incoming, *arrived))
    back, force = particles(incoming, middle, False)
    returned = exchange(back)
    final_state = call(
        functools.partial(fluid_kernel, False), shape(4, ELEMS, 512), name="last_fluid"
    )(middle, force, *tables, faces, *arrived)
    final_speeds = call(final_kernel, shape(3, BIN), name="final")(returned, code_two)
    return (final_state, final_speeds)


def solution(mesh):
    in_specs = (
        P(None, ("gx", "gy", "gz"), None),
        P(("gx", "gy", "gz"), None),
        P(("gx", "gy", "gz")),
        P(None, ("gx", "gy", "gz")),
        P(("gx", "gy", "gz")),
        P(None, ("gx", "gy", "gz")),
        P(None, ("gx", "gy", "gz")),
        P(("gx", "gy", "gz")),
        P(),
    )
    out_specs = (P(None, ("gx", "gy", "gz"), None), P(None, ("gx", "gy", "gz")))
    return jax.shard_map(local, mesh=mesh, in_specs=in_specs, out_specs=out_specs, check_vma=False)
```

```python
import functools

import jax
import jax.numpy as jnp
import numpy as np
from jax import lax
from jax.experimental import pallas as pl
from jax.experimental.pallas import tpu as pltpu
from jax.sharding import PartitionSpec as P

node_points = -np.cos(np.pi * np.arange(8) / 7.0)
step_time = 0.1
viscosity = 0.002
penalty = 0.25
loading = 0.5
heating = 0.5

ELEMS = 64
OWNERS = 64
BIN = 2048
CAP = 64
ROWS = OWNERS * CAP // 128
CHUNK_ROWS = 4
CHUNK = 128 * CHUNK_ROWS
BODY = 8

f32 = jnp.float32
bf16 = jnp.bfloat16
i32 = jnp.int32


def laplace_table():
    differences = node_points[:, None] - node_points[None, :] + np.eye(8)
    weights = 1.0 / np.prod(differences, axis=1)
    derivative = weights[None, :] / weights[:, None] / differences
    derivative = derivative * (1.0 - np.eye(8))
    derivative = derivative - np.eye(8) * derivative.sum(axis=1)[:, None]
    second = derivative @ derivative
    identity = np.eye(8)
    operator = np.kron(np.kron(second, identity), identity)
    operator = operator + np.kron(np.kron(identity, second), identity)
    operator = operator + np.kron(np.kron(identity, identity), second)
    return operator.T


def face_table():
    selection = np.zeros((512, 384))
    for face_side in range(6):
        edge_value = 0 if face_side % 2 == 0 else 7
        for row_node in range(8):
            for col_node in range(8):
                if face_side < 2:
                    node_index = (edge_value * 8 + row_node) * 8 + col_node
                elif face_side < 4:
                    node_index = (row_node * 8 + edge_value) * 8 + col_node
                else:
                    node_index = (row_node * 8 + col_node) * 8 + edge_value
                selection[node_index, face_side * 64 + row_node * 8 + col_node] = 1.0
    return selection


def face_select():
    col = iota((1, 384), 1)
    side, first, second = col >> 6, (col >> 3) & 7, col & 7
    edge = (side & 1) * 7
    node_a = edge * 64 + first * 8 + second
    node_b = first * 64 + edge * 8 + second
    node_c = first * 64 + second * 8 + edge
    node = jnp.where(side < 2, node_a, jnp.where(side < 4, node_b, node_c))
    return jnp.where(iota((512, 384), 0) == node, 1.0, 0.0).astype(bf16)


def iota(shape, axis):
    return lax.broadcasted_iota(i32, shape, axis)


def split(x):
    high = x.astype(bf16)
    return high, (x - high.astype(f32)).astype(bf16)


def split_row(x):
    high = x.astype(bf16).astype(f32)
    return high, x - high


def dot(a, b):
    return jnp.dot(a, b, preferred_element_type=f32)


def dot_nt(a, b):
    return lax.dot_general(a, b, (((1,), (1,)), ((), ())), preferred_element_type=f32)


def rank_in_owner(owner):
    width = 256
    upto = jnp.where(iota((width, width), 0) <= iota((width, width), 1), 1.0, 0.0).astype(bf16)
    table = jnp.concatenate([upto, jnp.ones((width, width), bf16)], axis=0)
    before = jnp.zeros((OWNERS, width), f32)
    ranks = []
    for start in range(0, BIN, width):
        here = iota((OWNERS, width), 0) == owner[:, start : start + width]
        marks = jnp.where(here, 1.0, 0.0)
        counts = dot(jnp.concatenate([marks, before], axis=1).astype(bf16), table)
        ranks.append(jnp.sum(jnp.where(here, counts, 0.0), axis=0, keepdims=True) - 1.0)
        before = before + marks
    return jnp.concatenate(ranks, axis=1)


def thick(row, rows):
    sixteen = jnp.broadcast_to(row, (16, row.shape[1])).astype(bf16)
    return jnp.concatenate([sixteen] * (rows // 16), axis=0)


def one_hot(index, rows):
    return jnp.where(iota((rows, index.shape[1]), 0) == index, 1.0, 0.0).astype(bf16)


def scatter_slots(out_ref, owner, rank, values):
    owned = one_hot(owner, OWNERS)
    placed = one_hot(rank, CAP)
    for first in range(0, len(values), 4):
        highs, lows = [], []
        for value in values[first : first + 4]:
            high, low = split_row(value)
            highs.append(placed * thick(high, CAP))
            lows.append(placed * thick(low, CAP))
        out = dot_nt(owned, jnp.concatenate(highs, axis=0)) + dot_nt(
            owned, jnp.concatenate(lows, axis=0)
        )
        out_ref[:, first // 2, :] = out[:, :128]
        out_ref[:, first // 2 + 1, :] = out[:, 128:]


def gather_slots(blocks, owner, lane_hot):
    high, low = split(jnp.concatenate(blocks, axis=0))
    total = dot(jnp.concatenate([high, low], axis=1), jnp.concatenate([lane_hot] * 2, axis=0))
    owned = iota((OWNERS, BIN), 0) == owner
    return [
        jnp.sum(jnp.where(owned, total[k * OWNERS : (k + 1) * OWNERS], 0.0), axis=0, keepdims=True)
        for k in range(len(blocks))
    ]


def send_kernel(cell_ref, coord_ref, speed_ref, rate_ref, out_ref, code_ref):
    cell = cell_ref[...]
    owner = (cell >> 6) & (OWNERS - 1)
    element = (cell & (ELEMS - 1)).astype(f32)
    rank = rank_in_owner(owner)
    code_ref[0:1, :] = owner.astype(f32) * float(CAP) + rank
    code_ref[1:2, :] = rate_ref[...]
    values = [
        element,
        speed_ref[0:1, :],
        coord_ref[0:1, :],
        speed_ref[1:2, :],
        coord_ref[1:2, :],
        speed_ref[2:3, :],
        coord_ref[2:3, :],
        rate_ref[...],
    ]
    scatter_slots(out_ref, owner, rank.astype(i32), values)


def resend_kernel(cut_ref, back_ref, moved_ref, cell_ref, code_ref, coord_ref, out_ref):
    first_code = moved_ref[0:1, :].astype(i32)
    rate = moved_ref[1:2, :]
    part = jnp.where(iota((1, BIN), 1) + cut_ref[0] >= BIN, CAP, 0)
    lane_hot = one_hot((first_code & (CAP - 1)) + part, 128)
    speeds = gather_slots([back_ref[:, k, :] for k in range(3)], first_code >> 6, lane_hot)
    element = (cell_ref[...] & (ELEMS - 1)).astype(f32)
    code = code_ref[...]
    values = [
        element,
        speeds[0],
        coord_ref[0:1, :],
        speeds[1],
        coord_ref[1:2, :],
        speeds[2],
        coord_ref[2:3, :],
        rate,
    ]
    scatter_slots(out_ref, code >> 6, code & (CAP - 1), values)


def final_kernel(back_ref, code_ref, out_ref):
    code = code_ref[...]
    lane_hot = jnp.concatenate([one_hot(code & (CAP - 1), CAP)] * 2, axis=0)
    left = iota((OWNERS, 128), 1) < 64
    pair, last = back_ref[:, 0, :], back_ref[:, 1, :]
    blocks = [jnp.where(left, pair, 0.0), jnp.where(left, 0.0, pair), jnp.where(left, last, 0.0)]
    speeds = gather_slots(blocks, code >> 6, lane_hot)
    for k in range(3):
        out_ref[k : k + 1, :] = speeds[k]


def column(values):
    row = iota((8, 1), 0)
    result = jnp.zeros((8, 1), f32)
    for index, value in enumerate(values):
        result = jnp.where(row == index, float(value), result)
    return result


def lagrange(x):
    gaps = node_points[:, None] - node_points[None, :] + np.eye(8)
    one = pltpu.roll(x - column(node_points), 1, 0)
    two = one * pltpu.roll(one, 1, 0)
    four = two * pltpu.roll(two, 2, 0)
    last = pltpu.roll(one, 6, 0) * column(1.0 / np.prod(gaps, axis=1))
    return four * pltpu.roll(two, 4, 0) * last


def basis(coords, pair_ref, weight_ref):
    first, second, third = [lagrange(x) for x in coords]
    for a in range(8):
        pair_ref[8 * a : 8 * a + 8, :] = first[a : a + 1, :] * second
    for i in range(32):
        piece = jnp.concatenate(
            [pair_ref[2 * i + h : 2 * i + h + 1, :] * third for h in range(2)], axis=0
        )
        weight_ref[16 * i : 16 * i + 16, :], weight_ref[512 + 16 * i : 528 + 16 * i, :] = split(piece)


def along(rows, k):
    return jnp.concatenate([rows[i, k : k + 1, :] for i in range(CHUNK_ROWS)], axis=1)


def particle_kernel(shift, incoming_ref, state_ref, back_ref, force_ref, even_ref, odd_ref, fresh_ref, state_scr, pair_refs, weight_refs, source_refs, total_ref):
    low, high = incoming_ref[0:ROWS], incoming_ref[ROWS : 2 * ROWS]
    left = iota(low.shape, 2) < 64
    even_ref[...] = jnp.where(left, low, pltpu.roll(high, 64, 2))
    odd_ref[...] = jnp.where(left, pltpu.roll(low, 64, 2), high)
    high, low = split(state_ref[0:3].reshape(3 * ELEMS, 512))
    state_scr[0 : 3 * ELEMS] = high
    state_scr[3 * ELEMS :] = low
    fresh_ref[:, 3:4, :] = jnp.zeros((ROWS + 1, 1, 128), f32)

    total_ref[...] = jnp.zeros_like(total_ref)

    def one(start, weight_ref, source_ref, pair_ref):
        even = even_ref[pl.ds(start, CHUNK_ROWS)]
        odd = odd_ref[pl.ds(start, CHUNK_ROWS)]
        basis([along(even, k) for k in (1, 2, 3)], pair_ref, weight_ref)
        wide = dot(state_scr[...], weight_ref[0:512])
        rest = dot(state_scr[0 : 3 * ELEMS], weight_ref[512:1024])
        element = along(even, 0).astype(i32)
        here = iota((ELEMS, CHUNK), 0) == element
        rates = along(odd, 3)
        squares = None
        fresh, sources = [], []
        for k in range(3):
            rows = slice(k * ELEMS, (k + 1) * ELEMS)
            lower = slice((k + 3) * ELEMS, (k + 4) * ELEMS)
            picked = jnp.where(here, wide[rows] + wide[lower] + rest[rows], 0.0)
            speed = along(odd, k)
            offset = jnp.sum(picked, axis=0, keepdims=True) - speed
            accel = rates * offset
            squares = offset * offset if squares is None else squares + offset * offset
            sources.append(accel)
            fresh.append(speed + step_time * accel)
        sources.append(rates * squares)
        for i in range(CHUNK_ROWS):
            for k in range(3):
                fresh_ref[start + i, k : k + 1, :] = fresh[k][:, i * 128 : (i + 1) * 128]
        hot = one_hot(element, ELEMS)
        for k in range(4):
            high, low = split_row(sources[k])
            source_ref[0, k * ELEMS : (k + 1) * ELEMS] = hot * thick(high, ELEMS)
            source_ref[1, k * ELEMS : (k + 1) * ELEMS] = hot * thick(low, ELEMS)

    def push(weight_ref, source_ref):
        wide = dot_nt(weight_ref[...], source_ref[0])
        total_ref[...] += wide[:512] + wide[512:] + dot_nt(weight_ref[0:512], source_ref[1])

    def visit(index, carry):
        for h in range(BODY):
            one((index * BODY + h) * CHUNK_ROWS, weight_refs.at[h], source_refs.at[h], pair_refs.at[h])
        for h in range(BODY):
            push(weight_refs.at[h], source_refs.at[h])
        return carry

    lax.fori_loop(0, ROWS // CHUNK_ROWS // BODY, visit, 0)
    fresh = fresh_ref[0:ROWS]
    if shift:
        fresh_ref[ROWS] = pltpu.roll(fresh_ref[0], 64, 1)
        after = fresh_ref[1 : ROWS + 1]
        left = iota(fresh.shape, 2) < 64
        back_ref[0:ROWS] = jnp.where(left, fresh, pltpu.roll(after, 64, 2))
        back_ref[ROWS : 2 * ROWS] = jnp.where(left, pltpu.roll(fresh, 64, 2), after)
    else:
        turned = pltpu.roll(fresh, 64, 2)
        left = iota((ROWS, 1, 128), 2) < 64
        back_ref[0:ROWS, 0:1, :] = jnp.where(left, fresh[:, 0:1, :], turned[:, 1:2, :])
        back_ref[0:ROWS, 1:2, :] = fresh[:, 2:3, :]
        back_ref[ROWS : 2 * ROWS, 0:1, :] = jnp.where(left, turned[:, 0:1, :], fresh[:, 1:2, :])
        back_ref[ROWS : 2 * ROWS, 1:2, :] = turned[:, 2:3, :]
    force_ref[...] = total_ref[...].T


def pick_faces(state, select, chosen_ref, faces_ref, send_refs):
    high, low = split(state)
    picked = dot(jnp.concatenate([high, low], axis=0), select)
    picked = picked[: 4 * ELEMS] + picked[4 * ELEMS :]
    left = iota((ELEMS, 128), 1) < 64
    for pair in range(3):
        tiles = [picked[k * ELEMS : (k + 1) * ELEMS, pair * 128 : (pair + 1) * 128] for k in range(4)]
        turned = [pltpu.roll(tile, 64, 1) for tile in tiles]
        lower = [jnp.where(left, tiles[k], turned[k + 1]) for k in (0, 2)]
        upper = [jnp.where(left, turned[k], tiles[k + 1]) for k in (0, 2)]
        for side, parts in ((2 * pair, lower), (2 * pair + 1, upper)):
            face = jnp.concatenate(parts, axis=1)
            faces_ref[side] = face
            face_high, face_low = split(face)
            send_refs[side][...] = dot(chosen_ref[side], face_high) + dot(chosen_ref[side], face_low)


def links_kernel(device_ref, state_ref, near_t_ref, cell_ref, code_ref, own_ref, far_ref, chosen_ref, faces_ref, *send_refs):
    device = device_ref[0]
    near_t = near_t_ref[...].astype(f32)
    near = jnp.concatenate([near_t, near_t[0:2]], axis=0).T.astype(i32)
    for side in range(6):
        target = near[:, side : side + 1]
        target_t = near_t_ref[side : side + 1, :]
        outside = (target >> 6) != device
        outside_t = (target_t >> 6) != device
        remote = (target >= 0) & outside
        remote_t = (target_t >= 0) & outside_t
        slot = jnp.where(outside, -1, target & (ELEMS - 1))
        own = (iota((ELEMS, 2 * ELEMS), 1) & (ELEMS - 1)) == slot
        own_ref[side] = jnp.where(own, 1.0, 0.0).astype(bf16)
        key = jnp.where(remote, target & (ELEMS - 1), ELEMS)
        key_t = jnp.where(remote_t, target_t & (ELEMS - 1), ELEMS)
        rank = jnp.sum(jnp.where(key_t < key, 1.0, 0.0), axis=1, keepdims=True)
        rank = jnp.where(remote, rank, -1.0)
        far = (iota((ELEMS, 32), 1) & 15).astype(f32) == rank
        far_ref[side] = jnp.where(far, 1.0, 0.0).astype(bf16)
        before = (iota((ELEMS, ELEMS), 0) < iota((ELEMS, ELEMS), 1)) & outside
        rank = jnp.sum(jnp.where(before, 1.0, 0.0), axis=0, keepdims=True)
        rank = jnp.where(outside_t, rank, -1.0)
        chosen = iota((16, ELEMS), 0).astype(f32) == rank
        chosen_ref[side] = jnp.where(chosen, 1.0, 0.0).astype(bf16)
    pick_faces(state_ref[...].reshape(4 * ELEMS, 512), face_select(), chosen_ref, faces_ref, send_refs)
    owner = (cell_ref[...] >> 6) & (OWNERS - 1)
    code_ref[...] = owner * CAP + rank_in_owner(owner).astype(i32)


def fluid_kernel(again, state_ref, force_ref, own_ref, far_ref, lap_high_ref, lap_low_ref, keep_ref, faces_ref, *refs):
    halo_refs, refs = refs[:6], refs[6:]
    if again:
        chosen_ref, out_ref, next_ref = refs[:3]
        send_refs = refs[3:]
    else:
        (out_ref,) = refs
    partners = []
    for side in range(6):
        face = jnp.concatenate(split(faces_ref[side ^ 1]), axis=0)
        halo = jnp.concatenate(split(halo_refs[side][...]), axis=0)
        partners.append(dot(own_ref[side], face) + dot(far_ref[side], halo))
    left = iota((ELEMS, 128), 1) < 64
    turned = [[pltpu.roll(p[:, h * 128 : (h + 1) * 128], 64, 1) for h in range(2)] for p in partners]
    joined = []
    for k in range(4):
        h = k // 2
        row = []
        for pair in range(3):
            lower, upper = partners[2 * pair], partners[2 * pair + 1]
            lanes = slice(h * 128, (h + 1) * 128)
            if k % 2 == 0:
                row.append(jnp.where(left, lower[:, lanes], turned[2 * pair + 1][h]))
            else:
                row.append(jnp.where(left, turned[2 * pair][h], upper[:, lanes]))
        joined.append(jnp.concatenate(row, axis=1))
    high, low = split(jnp.concatenate(joined, axis=0))
    select = face_select()
    spread = dot_nt(jnp.concatenate([high, low], axis=0), select)
    spread = spread[: 4 * ELEMS] + spread[4 * ELEMS :]
    state = state_ref[...].reshape(4 * ELEMS, 512)
    high, low = split(state)
    wide = dot(jnp.concatenate([high, low], axis=0), lap_high_ref[...])
    laplace = wide[: 4 * ELEMS] + wide[4 * ELEMS :] + dot(high, lap_low_ref[...])
    result = state * keep_ref[...] + viscosity * laplace + penalty * spread
    row = iota((4 * ELEMS, 1), 0)
    result = result + jnp.where(row < 3 * ELEMS, -loading, heating) * force_ref[...]
    out_ref[...] = result.reshape(4, ELEMS, 512)
    if again:
        pick_faces(result, select, chosen_ref, next_ref, send_refs)


def call(kernel, shapes, scratch=(), scalars=0, name=None, near=()):
    vmem = pl.BlockSpec(memory_space=pltpu.VMEM)
    smem = pl.BlockSpec(memory_space=pltpu.SMEM)

    def run(*args):
        args = list(args)
        for place in near:
            args[place] = pltpu.with_memory_space_constraint(args[place], pltpu.VMEM)
        return pl.pallas_call(
            kernel,
            out_shape=shapes,
            in_specs=[smem] * scalars + [vmem] * (len(args) - scalars),
            out_specs=jax.tree.map(lambda _: vmem, shapes),
            scratch_shapes=list(scratch),
            name=name,
        )(*args)

    return run


def close(*dims, dtype=f32):
    return pltpu.VMEM(dims, dtype)


def shape(*dims, dtype=f32):
    return jax.ShapeDtypeStruct(dims, dtype)


def local(field, neighbours, cell_one, ref_one, cell_two, ref_two, velocity, rate, cut):
    device = lax.axis_index(("gx", "gy", "gz")).astype(i32).reshape(1)
    near_t = neighbours.T
    lap = laplace_table()
    lap_high = jnp.asarray(lap, bf16)
    lap_low = jnp.asarray(lap - np.asarray(np.asarray(lap, bf16), np.float64), bf16)
    keep = jnp.asarray(1.0 - penalty * face_table().sum(axis=1), f32)[None]
    row_one, row_two = cell_one[None], cell_two[None]
    slots = close(OWNERS, 4, 128)

    def exchange(block):
        return lax.all_to_all(block, ("gy", "gz"), split_axis=0, concat_axis=0, tiled=True)

    def neighbour_faces(sends):
        arrived = [None] * 6
        for axis_index, axis in enumerate(("gx", "gy", "gz")):
            count = lax.axis_size(axis)
            span = count if axis == "gz" else count - 1
            up = [(i, (i + 1) % count) for i in range(span)]
            arrived[2 * axis_index] = lax.ppermute(sends[2 * axis_index + 1], axis, up)
            arrived[2 * axis_index + 1] = lax.ppermute(
                sends[2 * axis_index], axis, [(b, a) for a, b in up]
            )
        return arrived

    face_shapes = [close(6, ELEMS, 256)] + [close(16, 256)] * 6

    def particles(incoming, state, shift):
        back = slots if shift else close(OWNERS, 2, 128)
        return call(
            functools.partial(particle_kernel, shift),
            [back, close(4 * ELEMS, 512)],
            scratch=[
                pltpu.VMEM((ROWS, 4, 128), f32),
                pltpu.VMEM((ROWS, 4, 128), f32),
                pltpu.VMEM((ROWS + 1, 4, 128), f32),
                pltpu.VMEM((6 * ELEMS, 512), bf16),
                pltpu.VMEM((BODY, 64, CHUNK), f32),
                pltpu.VMEM((BODY, 1024, CHUNK), bf16),
                pltpu.VMEM((BODY, 2, 4 * ELEMS, CHUNK), bf16),
                pltpu.VMEM((512, 4 * ELEMS), f32),
            ],
            name="particles",
            near=(0, 1),
        )(incoming, state)

    outgoing, code_rate = call(send_kernel, [slots, shape(2, BIN)], name="send")(
        row_one, ref_one, velocity, rate[None]
    )
    incoming = exchange(outgoing)
    owners = lax.axis_size("gy") * lax.axis_size("gz")
    following = lax.ppermute(
        code_rate, ("gy", "gz"), [((i + 1) % owners, i) for i in range(owners)]
    )
    moved = lax.dynamic_slice_in_dim(
        jnp.concatenate([code_rate, following], axis=1), cut[0], BIN, 1
    )
    hots = [
        shape(6, ELEMS, 2 * ELEMS, dtype=bf16),
        shape(6, ELEMS, 32, dtype=bf16),
        shape(6, 16, ELEMS, dtype=bf16),
    ]
    code_two, own, far, chosen, faces, *sends = call(
        links_kernel, [shape(1, BIN, dtype=i32)] + hots + face_shapes, scalars=1, name="links"
    )(device, field, near_t, row_two)
    arrived = neighbour_faces(sends)
    tables = (own, far, lap_high, lap_low, keep)

    incoming, moved, *arrived = lax.optimization_barrier((incoming, moved, *arrived))
    back, force = particles(incoming, field, True)
    returned = exchange(back)
    middle, faces, *sends = call(
        functools.partial(fluid_kernel, True), [close(4, ELEMS, 512)] + face_shapes, name="fluid", near=(1, 7, 8, 9, 10, 11, 12, 13)
    )(field, force, *tables, faces, *arrived, chosen)
    returned, middle, *sends = lax.optimization_barrier((returned, middle, *sends))
    arrived = neighbour_faces(sends)
    outgoing = call(resend_kernel, slots, scalars=1, name="resend", near=(1, 2, 3, 4, 5))(
        cut, returned, moved, row_two, code_two, ref_two
    )
    incoming = exchange(outgoing)
    incoming, *arrived = lax.optimization_barrier((incoming, *arrived))
    back, force = particles(incoming, middle, False)
    returned = exchange(back)
    final_state = call(
        functools.partial(fluid_kernel, False), shape(4, ELEMS, 512), name="last_fluid", near=(0, 1, 7, 8, 9, 10, 11, 12, 13)
    )(middle, force, *tables, faces, *arrived)
    final_speeds = call(final_kernel, shape(3, BIN), name="final", near=(0, 1))(returned, code_two)
    return (final_state, final_speeds)


def solution(mesh):
    in_specs = (
        P(None, ("gx", "gy", "gz"), None),
        P(("gx", "gy", "gz"), None),
        P(("gx", "gy", "gz")),
        P(None, ("gx", "gy", "gz")),
        P(("gx", "gy", "gz")),
        P(None, ("gx", "gy", "gz")),
        P(None, ("gx", "gy", "gz")),
        P(("gx", "gy", "gz")),
        P(),
    )
    out_specs = (P(None, ("gx", "gy", "gz"), None), P(None, ("gx", "gy", "gz")))
    return jax.shard_map(local, mesh=mesh, in_specs=in_specs, out_specs=out_specs, check_vma=False)
```

```python
import functools

import jax
import jax.numpy as jnp
import numpy as np
from jax import lax
from jax.experimental import pallas as pl
from jax.experimental.pallas import tpu as pltpu
from jax.sharding import PartitionSpec as P


node_points = -np.cos(np.pi * np.arange(8) / 7.0)
step_time = 0.1
viscosity = 0.002
penalty = 0.25
loading = 0.5
heating = 0.5

ELEMS = 64
OWNERS = 64
BIN = 2048
CAP = 64
ROWS = OWNERS * CAP // 128
CHUNK_ROWS = 4
CHUNK = 128 * CHUNK_ROWS
BODY = 8

f32 = jnp.float32
bf16 = jnp.bfloat16
i32 = jnp.int32


def laplace_table():
    differences = node_points[:, None] - node_points[None, :] + np.eye(8)
    weights = 1.0 / np.prod(differences, axis=1)
    derivative = weights[None, :] / weights[:, None] / differences
    derivative = derivative * (1.0 - np.eye(8))
    derivative = derivative - np.eye(8) * derivative.sum(axis=1)[:, None]
    second = derivative @ derivative
    identity = np.eye(8)
    operator = np.kron(np.kron(second, identity), identity)
    operator = operator + np.kron(np.kron(identity, second), identity)
    operator = operator + np.kron(np.kron(identity, identity), second)
    return operator.T


def face_table():
    selection = np.zeros((512, 384))
    for face_side in range(6):
        edge_value = 0 if face_side % 2 == 0 else 7
        for row_node in range(8):
            for col_node in range(8):
                if face_side < 2:
                    node_index = (edge_value * 8 + row_node) * 8 + col_node
                elif face_side < 4:
                    node_index = (row_node * 8 + edge_value) * 8 + col_node
                else:
                    node_index = (row_node * 8 + col_node) * 8 + edge_value
                selection[node_index, face_side * 64 + row_node * 8 + col_node] = 1.0
    return selection


def face_select():
    col = iota((1, 384), 1)
    side, first, second = col >> 6, (col >> 3) & 7, col & 7
    edge = (side & 1) * 7
    node_a = edge * 64 + first * 8 + second
    node_b = first * 64 + edge * 8 + second
    node_c = first * 64 + second * 8 + edge
    node = jnp.where(side < 2, node_a, jnp.where(side < 4, node_b, node_c))
    return jnp.where(iota((512, 384), 0) == node, 1.0, 0.0).astype(bf16)


def iota(shape, axis):
    return lax.broadcasted_iota(i32, shape, axis)


def split(x):
    high = x.astype(bf16)
    return high, (x - high.astype(f32)).astype(bf16)


def split_row(x):
    high = x.astype(bf16).astype(f32)
    return high, x - high


def dot(a, b):
    return jnp.dot(a, b, preferred_element_type=f32)


def dot_nt(a, b):
    return lax.dot_general(a, b, (((1,), (1,)), ((), ())), preferred_element_type=f32)


def rank_in_owner(owner):
    width = 256
    upto = jnp.where(iota((width, width), 0) <= iota((width, width), 1), 1.0, 0.0).astype(bf16)
    table = jnp.concatenate([upto, jnp.ones((width, width), bf16)], axis=0)
    before = jnp.zeros((OWNERS, width), f32)
    ranks = []
    for start in range(0, BIN, width):
        here = iota((OWNERS, width), 0) == owner[:, start : start + width]
        marks = jnp.where(here, 1.0, 0.0)
        counts = dot(jnp.concatenate([marks, before], axis=1).astype(bf16), table)
        ranks.append(jnp.sum(jnp.where(here, counts, 0.0), axis=0, keepdims=True) - 1.0)
        before = before + marks
    return jnp.concatenate(ranks, axis=1)


def thick(row, rows):
    sixteen = jnp.broadcast_to(row, (16, row.shape[1])).astype(bf16)
    return jnp.concatenate([sixteen] * (rows // 16), axis=0)


def one_hot(index, rows):
    return jnp.where(iota((rows, index.shape[1]), 0) == index, 1.0, 0.0).astype(bf16)


def scatter_slots(out_ref, owner, rank, values):
    owned = one_hot(owner, OWNERS)
    placed = one_hot(rank, CAP)
    for first in range(0, len(values), 4):
        highs, lows = [], []
        for value in values[first : first + 4]:
            high, low = split_row(value)
            highs.append(placed * thick(high, CAP))
            lows.append(placed * thick(low, CAP))
        out = dot_nt(owned, jnp.concatenate(highs, axis=0)) + dot_nt(
            owned, jnp.concatenate(lows, axis=0)
        )
        out_ref[:, first // 2, :] = out[:, :128]
        out_ref[:, first // 2 + 1, :] = out[:, 128:]


def gather_slots(blocks, owner, lane_hot):
    high, low = split(jnp.concatenate(blocks, axis=0))
    total = dot(jnp.concatenate([high, low], axis=1), jnp.concatenate([lane_hot] * 2, axis=0))
    owned = iota((OWNERS, BIN), 0) == owner
    return [
        jnp.sum(jnp.where(owned, total[k * OWNERS : (k + 1) * OWNERS], 0.0), axis=0, keepdims=True)
        for k in range(len(blocks))
    ]


def send_kernel(cell_ref, coord_ref, speed_ref, rate_ref, out_ref, code_ref):
    cell = cell_ref[...]
    owner = (cell >> 6) & (OWNERS - 1)
    element = (cell & (ELEMS - 1)).astype(f32)
    rank = rank_in_owner(owner)
    code_ref[0:1, :] = owner.astype(f32) * float(CAP) + rank
    code_ref[1:2, :] = rate_ref[...]
    values = [
        element,
        speed_ref[0:1, :],
        coord_ref[0:1, :],
        speed_ref[1:2, :],
        coord_ref[1:2, :],
        speed_ref[2:3, :],
        coord_ref[2:3, :],
        rate_ref[...],
    ]
    scatter_slots(out_ref, owner, rank.astype(i32), values)


def resend_kernel(cut_ref, back_ref, moved_ref, cell_ref, code_ref, coord_ref, out_ref):
    first_code = moved_ref[0:1, :].astype(i32)
    rate = moved_ref[1:2, :]
    part = jnp.where(iota((1, BIN), 1) + cut_ref[0] >= BIN, CAP, 0)
    lane_hot = one_hot((first_code & (CAP - 1)) + part, 128)
    speeds = gather_slots([back_ref[:, k, :] for k in range(3)], first_code >> 6, lane_hot)
    element = (cell_ref[...] & (ELEMS - 1)).astype(f32)
    code = code_ref[...]
    values = [
        element,
        speeds[0],
        coord_ref[0:1, :],
        speeds[1],
        coord_ref[1:2, :],
        speeds[2],
        coord_ref[2:3, :],
        rate,
    ]
    scatter_slots(out_ref, code >> 6, code & (CAP - 1), values)


def final_kernel(back_ref, code_ref, out_ref):
    code = code_ref[...]
    lane_hot = jnp.concatenate([one_hot(code & (CAP - 1), CAP)] * 2, axis=0)
    left = iota((OWNERS, 128), 1) < 64
    pair, last = back_ref[:, 0, :], back_ref[:, 1, :]
    blocks = [jnp.where(left, pair, 0.0), jnp.where(left, 0.0, pair), jnp.where(left, last, 0.0)]
    speeds = gather_slots(blocks, code >> 6, lane_hot)
    for k in range(3):
        out_ref[k : k + 1, :] = speeds[k]


def column(values):
    row = iota((8, 1), 0)
    result = jnp.zeros((8, 1), f32)
    for index, value in enumerate(values):
        result = jnp.where(row == index, float(value), result)
    return result


def lagrange(x):
    gaps = node_points[:, None] - node_points[None, :] + np.eye(8)
    one = pltpu.roll(x - column(node_points), 1, 0)
    two = one * pltpu.roll(one, 1, 0)
    four = two * pltpu.roll(two, 2, 0)
    last = pltpu.roll(one, 6, 0) * column(1.0 / np.prod(gaps, axis=1))
    return four * pltpu.roll(two, 4, 0) * last


def basis(coords, pair_ref, weight_ref):
    first, second, third = [lagrange(x) for x in coords]
    for a in range(8):
        pair_ref[8 * a : 8 * a + 8, :] = first[a : a + 1, :] * second
    for i in range(32):
        piece = jnp.concatenate(
            [pair_ref[2 * i + h : 2 * i + h + 1, :] * third for h in range(2)], axis=0
        )
        weight_ref[16 * i : 16 * i + 16, :], weight_ref[512 + 16 * i : 528 + 16 * i, :] = split(piece)


def along(rows, k):
    return jnp.concatenate([rows[i, k : k + 1, :] for i in range(CHUNK_ROWS)], axis=1)


def particle_kernel(shift, incoming_ref, state_ref, back_ref, force_ref, even_ref, odd_ref, fresh_ref, state_scr, pair_refs, weight_refs, source_refs, total_ref):
    low, high = incoming_ref[0:ROWS], incoming_ref[ROWS : 2 * ROWS]
    left = iota(low.shape, 2) < 64
    even_ref[...] = jnp.where(left, low, pltpu.roll(high, 64, 2))
    odd_ref[...] = jnp.where(left, pltpu.roll(low, 64, 2), high)
    high, low = split(state_ref[0:3].reshape(3 * ELEMS, 512))
    state_scr[0 : 3 * ELEMS] = high
    state_scr[3 * ELEMS :] = low
    fresh_ref[:, 3:4, :] = jnp.zeros((ROWS + 1, 1, 128), f32)

    total_ref[...] = jnp.zeros_like(total_ref)

    def one(start, weight_ref, source_ref, pair_ref):
        even = even_ref[pl.ds(start, CHUNK_ROWS)]
        odd = odd_ref[pl.ds(start, CHUNK_ROWS)]
        basis([along(even, k) for k in (1, 2, 3)], pair_ref, weight_ref)
        wide = dot(state_scr[...], weight_ref[0:512])
        rest = dot(state_scr[0 : 3 * ELEMS], weight_ref[512:1024])
        element = along(even, 0).astype(i32)
        here = iota((ELEMS, CHUNK), 0) == element
        rates = along(odd, 3)
        squares = None
        fresh, sources = [], []
        for k in range(3):
            rows = slice(k * ELEMS, (k + 1) * ELEMS)
            lower = slice((k + 3) * ELEMS, (k + 4) * ELEMS)
            picked = jnp.where(here, wide[rows] + wide[lower] + rest[rows], 0.0)
            speed = along(odd, k)
            offset = jnp.sum(picked, axis=0, keepdims=True) - speed
            accel = rates * offset
            squares = offset * offset if squares is None else squares + offset * offset
            sources.append(accel)
            fresh.append(speed + step_time * accel)
        sources.append(rates * squares)
        for i in range(CHUNK_ROWS):
            for k in range(3):
                fresh_ref[start + i, k : k + 1, :] = fresh[k][:, i * 128 : (i + 1) * 128]
        hot = one_hot(element, ELEMS)
        for k in range(4):
            high, low = split_row(sources[k])
            source_ref[0, k * ELEMS : (k + 1) * ELEMS] = hot * thick(high, ELEMS)
            source_ref[1, k * ELEMS : (k + 1) * ELEMS] = hot * thick(low, ELEMS)

    def push(weight_ref, source_ref):
        wide = dot_nt(weight_ref[...], source_ref[0])
        total_ref[...] += wide[:512] + wide[512:] + dot_nt(weight_ref[0:512], source_ref[1])

    def visit(index, carry):
        for h in range(BODY):
            one((index * BODY + h) * CHUNK_ROWS, weight_refs.at[h], source_refs.at[h], pair_refs.at[h])
        for h in range(BODY):
            push(weight_refs.at[h], source_refs.at[h])
        return carry

    lax.fori_loop(0, ROWS // CHUNK_ROWS // BODY, visit, 0)
    fresh = fresh_ref[0:ROWS]
    if shift:
        fresh_ref[ROWS] = pltpu.roll(fresh_ref[0], 64, 1)
        after = fresh_ref[1 : ROWS + 1]
        left = iota(fresh.shape, 2) < 64
        back_ref[0:ROWS] = jnp.where(left, fresh, pltpu.roll(after, 64, 2))
        back_ref[ROWS : 2 * ROWS] = jnp.where(left, pltpu.roll(fresh, 64, 2), after)
    else:
        turned = pltpu.roll(fresh, 64, 2)
        left = iota((ROWS, 1, 128), 2) < 64
        back_ref[0:ROWS, 0:1, :] = jnp.where(left, fresh[:, 0:1, :], turned[:, 1:2, :])
        back_ref[0:ROWS, 1:2, :] = fresh[:, 2:3, :]
        back_ref[ROWS : 2 * ROWS, 0:1, :] = jnp.where(left, turned[:, 0:1, :], fresh[:, 1:2, :])
        back_ref[ROWS : 2 * ROWS, 1:2, :] = turned[:, 2:3, :]
    force_ref[...] = total_ref[...].T


def pick_faces(state, select, chosen_ref, faces_ref, send_refs):
    high, low = split(state)
    picked = dot(jnp.concatenate([high, low], axis=0), select)
    picked = picked[: 4 * ELEMS] + picked[4 * ELEMS :]
    left = iota((ELEMS, 128), 1) < 64
    for pair in range(3):
        tiles = [picked[k * ELEMS : (k + 1) * ELEMS, pair * 128 : (pair + 1) * 128] for k in range(4)]
        turned = [pltpu.roll(tile, 64, 1) for tile in tiles]
        lower = [jnp.where(left, tiles[k], turned[k + 1]) for k in (0, 2)]
        upper = [jnp.where(left, turned[k], tiles[k + 1]) for k in (0, 2)]
        for side, parts in ((2 * pair, lower), (2 * pair + 1, upper)):
            face = jnp.concatenate(parts, axis=1)
            faces_ref[side] = face
            face_high, face_low = split(face)
            send_refs[side][...] = dot(chosen_ref[side], face_high) + dot(chosen_ref[side], face_low)


def links_kernel(device_ref, state_ref, near_t_ref, chosen_ref, faces_ref, *send_refs):
    device = device_ref[0]
    near_t = near_t_ref[...].astype(f32)
    near = jnp.concatenate([near_t, near_t[0:2]], axis=0).T.astype(i32)
    for side in range(6):
        outside = (near[:, side : side + 1] >> 6) != device
        outside_t = (near_t_ref[side : side + 1, :] >> 6) != device
        before = (iota((ELEMS, ELEMS), 0) < iota((ELEMS, ELEMS), 1)) & outside
        rank = jnp.sum(jnp.where(before, 1.0, 0.0), axis=0, keepdims=True)
        rank = jnp.where(outside_t, rank, -1.0)
        chosen = iota((16, ELEMS), 0).astype(f32) == rank
        chosen_ref[side] = jnp.where(chosen, 1.0, 0.0).astype(bf16)
    pick_faces(state_ref[...].reshape(4 * ELEMS, 512), face_select(), chosen_ref, faces_ref, send_refs)


def tables_kernel(device_ref, near_t_ref, cell_ref, code_ref, own_ref, far_ref):
    device = device_ref[0]
    near_t = near_t_ref[...].astype(f32)
    near = jnp.concatenate([near_t, near_t[0:2]], axis=0).T.astype(i32)
    for side in range(6):
        target = near[:, side : side + 1]
        target_t = near_t_ref[side : side + 1, :]
        outside = (target >> 6) != device
        remote = (target >= 0) & outside
        remote_t = (target_t >= 0) & ((target_t >> 6) != device)
        slot = jnp.where(outside, -1, target & (ELEMS - 1))
        own = (iota((ELEMS, 2 * ELEMS), 1) & (ELEMS - 1)) == slot
        own_ref[side] = jnp.where(own, 1.0, 0.0).astype(bf16)
        key = jnp.where(remote, target & (ELEMS - 1), ELEMS)
        key_t = jnp.where(remote_t, target_t & (ELEMS - 1), ELEMS)
        rank = jnp.sum(jnp.where(key_t < key, 1.0, 0.0), axis=1, keepdims=True)
        rank = jnp.where(remote, rank, -1.0)
        far = (iota((ELEMS, 32), 1) & 15).astype(f32) == rank
        far_ref[side] = jnp.where(far, 1.0, 0.0).astype(bf16)
    owner = (cell_ref[...] >> 6) & (OWNERS - 1)
    code_ref[...] = owner * CAP + rank_in_owner(owner).astype(i32)


def fluid_kernel(again, state_ref, force_ref, own_ref, far_ref, lap_high_ref, lap_low_ref, keep_ref, faces_ref, *refs):
    halo_refs, refs = refs[:6], refs[6:]
    if again:
        chosen_ref, out_ref, next_ref = refs[:3]
        send_refs = refs[3:]
    else:
        (out_ref,) = refs
    partners = []
    for side in range(6):
        face = jnp.concatenate(split(faces_ref[side ^ 1]), axis=0)
        halo = jnp.concatenate(split(halo_refs[side][...]), axis=0)
        partners.append(dot(own_ref[side], face) + dot(far_ref[side], halo))
    left = iota((ELEMS, 128), 1) < 64
    turned = [[pltpu.roll(p[:, h * 128 : (h + 1) * 128], 64, 1) for h in range(2)] for p in partners]
    joined = []
    for k in range(4):
        h = k // 2
        row = []
        for pair in range(3):
            lower, upper = partners[2 * pair], partners[2 * pair + 1]
            lanes = slice(h * 128, (h + 1) * 128)
            if k % 2 == 0:
                row.append(jnp.where(left, lower[:, lanes], turned[2 * pair + 1][h]))
            else:
                row.append(jnp.where(left, turned[2 * pair][h], upper[:, lanes]))
        joined.append(jnp.concatenate(row, axis=1))
    high, low = split(jnp.concatenate(joined, axis=0))
    select = face_select()
    spread = dot_nt(jnp.concatenate([high, low], axis=0), select)
    spread = spread[: 4 * ELEMS] + spread[4 * ELEMS :]
    state = state_ref[...].reshape(4 * ELEMS, 512)
    high, low = split(state)
    wide = dot(jnp.concatenate([high, low], axis=0), lap_high_ref[...])
    laplace = wide[: 4 * ELEMS] + wide[4 * ELEMS :] + dot(high, lap_low_ref[...])
    result = state * keep_ref[...] + viscosity * laplace + penalty * spread
    row = iota((4 * ELEMS, 1), 0)
    result = result + jnp.where(row < 3 * ELEMS, -loading, heating) * force_ref[...]
    out_ref[...] = result.reshape(4, ELEMS, 512)
    if again:
        pick_faces(result, select, chosen_ref, next_ref, send_refs)


def call(kernel, shapes, scratch=(), scalars=0, near=()):
    vmem = pl.BlockSpec(memory_space=pltpu.VMEM)
    smem = pl.BlockSpec(memory_space=pltpu.SMEM)

    def run(*args):
        args = list(args)
        for place in near:
            args[place] = pltpu.with_memory_space_constraint(args[place], pltpu.VMEM)
        return pl.pallas_call(
            kernel,
            out_shape=shapes,
            in_specs=[smem] * scalars + [vmem] * (len(args) - scalars),
            out_specs=jax.tree.map(lambda _: vmem, shapes),
            scratch_shapes=list(scratch),
        )(*args)

    return run


def close(*dims, dtype=f32):
    return pltpu.VMEM(dims, dtype)


def shape(*dims, dtype=f32):
    return jax.ShapeDtypeStruct(dims, dtype)


def local(field, neighbours, cell_one, ref_one, cell_two, ref_two, velocity, rate, cut):
    device = lax.axis_index(("gx", "gy", "gz")).astype(i32).reshape(1)
    near_t = neighbours.T
    lap = laplace_table()
    lap_high = jnp.asarray(lap, bf16)
    lap_low = jnp.asarray(lap - np.asarray(np.asarray(lap, bf16), np.float64), bf16)
    keep = jnp.asarray(1.0 - penalty * face_table().sum(axis=1), f32)[None]
    row_one, row_two = cell_one[None], cell_two[None]
    slots = close(OWNERS, 4, 128)

    def exchange(block):
        return lax.all_to_all(block, ("gy", "gz"), split_axis=0, concat_axis=0, tiled=True)

    def neighbour_faces(sends):
        arrived = [None] * 6
        for axis_index, axis in enumerate(("gx", "gy", "gz")):
            count = lax.axis_size(axis)
            up = [(i, (i + 1) % count) for i in range(count)]
            arrived[2 * axis_index] = lax.ppermute(sends[2 * axis_index + 1], axis, up)
            arrived[2 * axis_index + 1] = lax.ppermute(
                sends[2 * axis_index], axis, [(b, a) for a, b in up]
            )
        return arrived

    face_shapes = [close(6, ELEMS, 256)] + [close(16, 256)] * 6

    def particles(incoming, state, shift):
        back = slots if shift else close(OWNERS, 2, 128)
        return call(
            functools.partial(particle_kernel, shift),
            [back, close(4 * ELEMS, 512)],
            scratch=[
                pltpu.VMEM((ROWS, 4, 128), f32),
                pltpu.VMEM((ROWS, 4, 128), f32),
                pltpu.VMEM((ROWS + 1, 4, 128), f32),
                pltpu.VMEM((6 * ELEMS, 512), bf16),
                pltpu.VMEM((BODY, 64, CHUNK), f32),
                pltpu.VMEM((BODY, 1024, CHUNK), bf16),
                pltpu.VMEM((BODY, 2, 4 * ELEMS, CHUNK), bf16),
                pltpu.VMEM((512, 4 * ELEMS), f32),
            ],
            near=(0, 1),
        )(incoming, state)

    outgoing, code_rate = call(send_kernel, [slots, shape(2, BIN)])(
        row_one, ref_one, velocity, rate[None]
    )
    incoming = exchange(outgoing)
    owners = lax.axis_size("gy") * lax.axis_size("gz")
    following = lax.ppermute(
        code_rate, ("gy", "gz"), [((i + 1) % owners, i) for i in range(owners)]
    )
    moved = lax.dynamic_slice_in_dim(
        jnp.concatenate([code_rate, following], axis=1), cut[0], BIN, 1
    )
    chosen, faces, *sends = call(
        links_kernel, [shape(6, 16, ELEMS, dtype=bf16)] + face_shapes, scalars=1
    )(device, field, near_t)
    arrived = neighbour_faces(sends)

    incoming, moved = lax.optimization_barrier((incoming, moved))
    back, force = particles(incoming, field, True)
    returned = exchange(back)
    force, near_t, row_two = lax.optimization_barrier((force, near_t, row_two))
    hots = [close(6, ELEMS, 2 * ELEMS, dtype=bf16), close(6, ELEMS, 32, dtype=bf16)]
    code_two, own, far = call(
        tables_kernel, [close(1, BIN, dtype=i32)] + hots, scalars=1, near=(1, 2)
    )(device, near_t, row_two)
    tables = (own, far, lap_high, lap_low, keep)
    middle, faces, *sends = call(
        functools.partial(fluid_kernel, True), [close(4, ELEMS, 512)] + face_shapes, near=(1, 2, 3, 7, 8, 9, 10, 11, 12, 13)
    )(field, force, *tables, faces, *arrived, chosen)
    returned, middle, *sends = lax.optimization_barrier((returned, middle, *sends))
    arrived = neighbour_faces(sends)
    outgoing = call(resend_kernel, slots, scalars=1, near=(1, 2, 3, 4, 5))(
        cut, returned, moved, row_two, code_two, ref_two
    )
    incoming = exchange(outgoing)
    back, force = particles(incoming, middle, False)
    returned = exchange(back)
    final_state = call(
        functools.partial(fluid_kernel, False), shape(4, ELEMS, 512), near=(0, 1, 2, 3, 7, 8, 9, 10, 11, 12, 13)
    )(middle, force, *tables, faces, *arrived)
    final_speeds = call(final_kernel, shape(3, BIN), near=(0, 1))(returned, code_two)
    return (final_state, final_speeds)


def solution(mesh):
    in_specs = (
        P(None, ("gx", "gy", "gz"), None),
        P(("gx", "gy", "gz"), None),
        P(("gx", "gy", "gz")),
        P(None, ("gx", "gy", "gz")),
        P(("gx", "gy", "gz")),
        P(None, ("gx", "gy", "gz")),
        P(None, ("gx", "gy", "gz")),
        P(("gx", "gy", "gz")),
        P(),
    )
    out_specs = (P(None, ("gx", "gy", "gz"), None), P(None, ("gx", "gy", "gz")))

    return jax.shard_map(local, mesh=mesh, in_specs=in_specs, out_specs=out_specs, check_vma=False)
```

```python
import functools

import jax
import jax.numpy as jnp
import numpy as np
from jax import lax
from jax.experimental import pallas as pl
from jax.experimental.pallas import tpu as pltpu
from jax.sharding import PartitionSpec as P


node_points = -np.cos(np.pi * np.arange(8) / 7.0)
step_time = 0.1
viscosity = 0.002
penalty = 0.25
loading = 0.5
heating = 0.5

ELEMS = 64
OWNERS = 64
BIN = 2048
CAP = 64
ROWS = OWNERS * CAP // 128
CHUNK_ROWS = 4
CHUNK = 128 * CHUNK_ROWS
BODY = 8

f32 = jnp.float32
bf16 = jnp.bfloat16
i32 = jnp.int32


def second_table():
    differences = node_points[:, None] - node_points[None, :] + np.eye(8)
    weights = 1.0 / np.prod(differences, axis=1)
    derivative = weights[None, :] / weights[:, None] / differences
    derivative = derivative * (1.0 - np.eye(8))
    derivative = derivative - np.eye(8) * derivative.sum(axis=1)[:, None]
    second = derivative @ derivative
    return second


def laplace_tables():
    second = second_table()
    plane = np.kron(second, np.eye(8)) + np.kron(np.eye(8), second)
    factors = np.zeros((32, 128))
    for s in range(4):
        for t in range(4):
            factors[8 * s + 2 * t, :64] = second[2 * s, 2 * t]
            factors[8 * s + 2 * t, 64:] = second[2 * s + 1, 2 * t + 1]
            factors[8 * s + 2 * t + 1, :64] = second[2 * s, 2 * t + 1]
            factors[8 * s + 2 * t + 1, 64:] = second[2 * s + 1, 2 * t]
    return np.kron(np.eye(2), plane).T, factors


def face_table():
    selection = np.zeros((512, 384))
    for face_side in range(6):
        edge_value = 0 if face_side % 2 == 0 else 7
        for row_node in range(8):
            for col_node in range(8):
                if face_side < 2:
                    node_index = (edge_value * 8 + row_node) * 8 + col_node
                elif face_side < 4:
                    node_index = (row_node * 8 + edge_value) * 8 + col_node
                else:
                    node_index = (row_node * 8 + col_node) * 8 + edge_value
                selection[node_index, face_side * 64 + row_node * 8 + col_node] = 1.0
    return selection


def face_select():
    col = iota((1, 384), 1)
    side, first, second = col >> 6, (col >> 3) & 7, col & 7
    edge = (side & 1) * 7
    node_a = edge * 64 + first * 8 + second
    node_b = first * 64 + edge * 8 + second
    node_c = first * 64 + second * 8 + edge
    node = jnp.where(side < 2, node_a, jnp.where(side < 4, node_b, node_c))
    return jnp.where(iota((512, 384), 0) == node, 1.0, 0.0).astype(bf16)


def iota(shape, axis):
    return lax.broadcasted_iota(i32, shape, axis)


def split(x):
    high = x.astype(bf16)
    return high, (x - high.astype(f32)).astype(bf16)


def split_row(x):
    high = x.astype(bf16).astype(f32)
    return high, x - high


def dot(a, b):
    return jnp.dot(a, b, preferred_element_type=f32)


def dot_nt(a, b):
    return lax.dot_general(a, b, (((1,), (1,)), ((), ())), preferred_element_type=f32)


def rank_in_owner(owner):
    width = 256
    upto = jnp.where(iota((width, width), 0) <= iota((width, width), 1), 1.0, 0.0).astype(bf16)
    table = jnp.concatenate([upto, jnp.ones((width, width), bf16)], axis=0)
    before = jnp.zeros((OWNERS, width), f32)
    ranks = []
    for start in range(0, BIN, width):
        here = iota((OWNERS, width), 0) == owner[:, start : start + width]
        marks = jnp.where(here, 1.0, 0.0)
        counts = dot(jnp.concatenate([marks, before], axis=1).astype(bf16), table)
        ranks.append(jnp.sum(jnp.where(here, counts, 0.0), axis=0, keepdims=True) - 1.0)
        before = before + marks
    return jnp.concatenate(ranks, axis=1)


def thick(row, rows):
    sixteen = jnp.broadcast_to(row, (16, row.shape[1])).astype(bf16)
    return jnp.concatenate([sixteen] * (rows // 16), axis=0)


def one_hot(index, rows):
    return jnp.where(iota((rows, index.shape[1]), 0) == index, 1.0, 0.0).astype(bf16)


def scatter_slots(out_ref, owner, rank, values):
    owned = one_hot(owner, OWNERS)
    placed = one_hot(rank, CAP)
    for first in range(0, len(values), 4):
        highs, lows = [], []
        for value in values[first : first + 4]:
            high, low = split_row(value)
            highs.append(placed * thick(high, CAP))
            lows.append(placed * thick(low, CAP))
        out = dot_nt(owned, jnp.concatenate(highs, axis=0)) + dot_nt(
            owned, jnp.concatenate(lows, axis=0)
        )
        out_ref[:, first // 2, :] = out[:, :128]
        out_ref[:, first // 2 + 1, :] = out[:, 128:]


def gather_slots(blocks, owner, lane_hot):
    high, low = split(jnp.concatenate(blocks, axis=0))
    total = dot(jnp.concatenate([high, low], axis=1), jnp.concatenate([lane_hot] * 2, axis=0))
    owned = iota((OWNERS, BIN), 0) == owner
    return [
        jnp.sum(jnp.where(owned, total[k * OWNERS : (k + 1) * OWNERS], 0.0), axis=0, keepdims=True)
        for k in range(len(blocks))
    ]


def send_kernel(cell_ref, coord_ref, speed_ref, rate_ref, out_ref, code_ref):
    cell = cell_ref[...]
    owner = (cell >> 6) & (OWNERS - 1)
    element = (cell & (ELEMS - 1)).astype(f32)
    rank = rank_in_owner(owner)
    code_ref[0:1, :] = owner.astype(f32) * float(CAP) + rank
    code_ref[1:2, :] = rate_ref[...]
    values = [
        element,
        speed_ref[0:1, :],
        coord_ref[0:1, :],
        speed_ref[1:2, :],
        coord_ref[1:2, :],
        speed_ref[2:3, :],
        coord_ref[2:3, :],
        rate_ref[...],
    ]
    scatter_slots(out_ref, owner, rank.astype(i32), values)


def resend_kernel(cut_ref, back_ref, moved_ref, cell_ref, code_ref, coord_ref, out_ref):
    first_code = moved_ref[0:1, :].astype(i32)
    rate = moved_ref[1:2, :]
    part = jnp.where(iota((1, BIN), 1) + cut_ref[0] >= BIN, CAP, 0)
    lane_hot = one_hot((first_code & (CAP - 1)) + part, 128)
    speeds = gather_slots([back_ref[:, k, :] for k in range(3)], first_code >> 6, lane_hot)
    element = (cell_ref[...] & (ELEMS - 1)).astype(f32)
    code = code_ref[...]
    values = [
        element,
        speeds[0],
        coord_ref[0:1, :],
        speeds[1],
        coord_ref[1:2, :],
        speeds[2],
        coord_ref[2:3, :],
        rate,
    ]
    scatter_slots(out_ref, code >> 6, code & (CAP - 1), values)


def final_kernel(back_ref, code_ref, out_ref):
    code = code_ref[...]
    lane_hot = jnp.concatenate([one_hot(code & (CAP - 1), CAP)] * 2, axis=0)
    left = iota((OWNERS, 128), 1) < 64
    pair, last = back_ref[:, 0, :], back_ref[:, 1, :]
    blocks = [jnp.where(left, pair, 0.0), jnp.where(left, 0.0, pair), jnp.where(left, last, 0.0)]
    speeds = gather_slots(blocks, code >> 6, lane_hot)
    for k in range(3):
        out_ref[k : k + 1, :] = speeds[k]


def column(values):
    row = iota((8, 1), 0)
    result = jnp.zeros((8, 1), f32)
    for index, value in enumerate(values):
        result = jnp.where(row == index, float(value), result)
    return result


def lagrange(x):
    gaps = node_points[:, None] - node_points[None, :] + np.eye(8)
    one = pltpu.roll(x - column(node_points), 1, 0)
    two = one * pltpu.roll(one, 1, 0)
    four = two * pltpu.roll(two, 2, 0)
    last = pltpu.roll(one, 6, 0) * column(1.0 / np.prod(gaps, axis=1))
    return four * pltpu.roll(two, 4, 0) * last


def basis(coords, pair_ref, weight_ref):
    first, second, third = [lagrange(x) for x in coords]
    for a in range(8):
        pair_ref[8 * a : 8 * a + 8, :] = first[a : a + 1, :] * second
    for i in range(32):
        piece = jnp.concatenate(
            [pair_ref[2 * i + h : 2 * i + h + 1, :] * third for h in range(2)], axis=0
        )
        weight_ref[16 * i : 16 * i + 16, :], weight_ref[512 + 16 * i : 528 + 16 * i, :] = split(piece)


def along(rows, k):
    return jnp.concatenate([rows[i, k : k + 1, :] for i in range(CHUNK_ROWS)], axis=1)


def particle_kernel(shift, incoming_ref, state_ref, back_ref, force_ref, even_ref, odd_ref, fresh_ref, state_scr, pair_refs, weight_refs, source_refs, total_ref):
    low, high = incoming_ref[0:ROWS], incoming_ref[ROWS : 2 * ROWS]
    left = iota(low.shape, 2) < 64
    even_ref[...] = jnp.where(left, low, pltpu.roll(high, 64, 2))
    odd_ref[...] = jnp.where(left, pltpu.roll(low, 64, 2), high)
    high, low = split(state_ref[0:3].reshape(3 * ELEMS, 512))
    state_scr[0 : 3 * ELEMS] = high
    state_scr[3 * ELEMS :] = low
    fresh_ref[:, 3:4, :] = jnp.zeros((ROWS + 1, 1, 128), f32)

    total_ref[...] = jnp.zeros_like(total_ref)

    def one(start, weight_ref, source_ref, pair_ref):
        even = even_ref[pl.ds(start, CHUNK_ROWS)]
        odd = odd_ref[pl.ds(start, CHUNK_ROWS)]
        basis([along(even, k) for k in (1, 2, 3)], pair_ref, weight_ref)
        wide = dot(state_scr[...], weight_ref[0:512])
        rest = dot(state_scr[0 : 3 * ELEMS], weight_ref[512:1024])
        element = along(even, 0).astype(i32)
        here = iota((ELEMS, CHUNK), 0) == element
        rates = along(odd, 3)
        squares = None
        fresh, sources = [], []
        for k in range(3):
            rows = slice(k * ELEMS, (k + 1) * ELEMS)
            lower = slice((k + 3) * ELEMS, (k + 4) * ELEMS)
            picked = jnp.where(here, wide[rows] + wide[lower] + rest[rows], 0.0)
            speed = along(odd, k)
            offset = jnp.sum(picked, axis=0, keepdims=True) - speed
            accel = rates * offset
            squares = offset * offset if squares is None else squares + offset * offset
            sources.append(accel)
            fresh.append(speed + step_time * accel)
        sources.append(rates * squares)
        for i in range(CHUNK_ROWS):
            for k in range(3):
                fresh_ref[start + i, k : k + 1, :] = fresh[k][:, i * 128 : (i + 1) * 128]
        hot = one_hot(element, ELEMS)
        for k in range(4):
            high, low = split_row(sources[k])
            source_ref[0, k * ELEMS : (k + 1) * ELEMS] = hot * thick(high, ELEMS)
            source_ref[1, k * ELEMS : (k + 1) * ELEMS] = hot * thick(low, ELEMS)

    def push(weight_ref, source_ref):
        wide = dot_nt(weight_ref[...], source_ref[0])
        total_ref[...] += wide[:512] + wide[512:] + dot_nt(weight_ref[0:512], source_ref[1])

    def visit(index, carry):
        for h in range(BODY):
            one((index * BODY + h) * CHUNK_ROWS, weight_refs.at[h], source_refs.at[h], pair_refs.at[h])
        for h in range(BODY):
            push(weight_refs.at[h], source_refs.at[h])
        return carry

    lax.fori_loop(0, ROWS // CHUNK_ROWS // BODY, visit, 0)
    fresh = fresh_ref[0:ROWS]
    if shift:
        fresh_ref[ROWS] = pltpu.roll(fresh_ref[0], 64, 1)
        after = fresh_ref[1 : ROWS + 1]
        left = iota(fresh.shape, 2) < 64
        back_ref[0:ROWS] = jnp.where(left, fresh, pltpu.roll(after, 64, 2))
        back_ref[ROWS : 2 * ROWS] = jnp.where(left, pltpu.roll(fresh, 64, 2), after)
    else:
        turned = pltpu.roll(fresh, 64, 2)
        left = iota((ROWS, 1, 128), 2) < 64
        back_ref[0:ROWS, 0:1, :] = jnp.where(left, fresh[:, 0:1, :], turned[:, 1:2, :])
        back_ref[0:ROWS, 1:2, :] = fresh[:, 2:3, :]
        back_ref[ROWS : 2 * ROWS, 0:1, :] = jnp.where(left, turned[:, 0:1, :], fresh[:, 1:2, :])
        back_ref[ROWS : 2 * ROWS, 1:2, :] = turned[:, 2:3, :]
    force_ref[...] = total_ref[...].T


def pick_faces(state, select, chosen_ref, faces_ref, send_refs):
    high, low = split(state)
    picked = dot(jnp.concatenate([high, low], axis=0), select)
    picked = picked[: 4 * ELEMS] + picked[4 * ELEMS :]
    left = iota((ELEMS, 128), 1) < 64
    for pair in range(3):
        tiles = [picked[k * ELEMS : (k + 1) * ELEMS, pair * 128 : (pair + 1) * 128] for k in range(4)]
        turned = [pltpu.roll(tile, 64, 1) for tile in tiles]
        lower = [jnp.where(left, tiles[k], turned[k + 1]) for k in (0, 2)]
        upper = [jnp.where(left, turned[k], tiles[k + 1]) for k in (0, 2)]
        for side, parts in ((2 * pair, lower), (2 * pair + 1, upper)):
            face = jnp.concatenate(parts, axis=1)
            faces_ref[side] = face
            face_high, face_low = split(face)
            send_refs[side][...] = dot(chosen_ref[side], face_high) + dot(chosen_ref[side], face_low)


def links_kernel(device_ref, state_ref, near_t_ref, chosen_ref, faces_ref, *send_refs):
    device = device_ref[0]
    near_t = near_t_ref[...].astype(f32)
    near = jnp.concatenate([near_t, near_t[0:2]], axis=0).T.astype(i32)
    for side in range(6):
        outside = (near[:, side : side + 1] >> 6) != device
        outside_t = (near_t_ref[side : side + 1, :] >> 6) != device
        before = (iota((ELEMS, ELEMS), 0) < iota((ELEMS, ELEMS), 1)) & outside
        rank = jnp.sum(jnp.where(before, 1.0, 0.0), axis=0, keepdims=True)
        rank = jnp.where(outside_t, rank, -1.0)
        chosen = iota((16, ELEMS), 0).astype(f32) == rank
        chosen_ref[side] = jnp.where(chosen, 1.0, 0.0).astype(bf16)
    pick_faces(state_ref[...].reshape(4 * ELEMS, 512), face_select(), chosen_ref, faces_ref, send_refs)


def tables_kernel(device_ref, near_t_ref, cell_ref, code_ref, own_ref, far_ref):
    device = device_ref[0]
    near_t = near_t_ref[...].astype(f32)
    near = jnp.concatenate([near_t, near_t[0:2]], axis=0).T.astype(i32)
    for side in range(6):
        target = near[:, side : side + 1]
        target_t = near_t_ref[side : side + 1, :]
        outside = (target >> 6) != device
        remote = (target >= 0) & outside
        remote_t = (target_t >= 0) & ((target_t >> 6) != device)
        slot = jnp.where(outside, -1, target & (ELEMS - 1))
        own = (iota((ELEMS, 2 * ELEMS), 1) & (ELEMS - 1)) == slot
        own_ref[side] = jnp.where(own, 1.0, 0.0).astype(bf16)
        key = jnp.where(remote, target & (ELEMS - 1), ELEMS)
        key_t = jnp.where(remote_t, target_t & (ELEMS - 1), ELEMS)
        rank = jnp.sum(jnp.where(key_t < key, 1.0, 0.0), axis=1, keepdims=True)
        rank = jnp.where(remote, rank, -1.0)
        far = (iota((ELEMS, 32), 1) & 15).astype(f32) == rank
        far_ref[side] = jnp.where(far, 1.0, 0.0).astype(bf16)
    owner = (cell_ref[...] >> 6) & (OWNERS - 1)
    code_ref[...] = owner * CAP + rank_in_owner(owner).astype(i32)


def fluid_kernel(again, state_ref, force_ref, own_ref, far_ref, plane_ref, factor_ref, keep_ref, faces_ref, *refs):
    halo_refs, refs = refs[:6], refs[6:]
    if again:
        chosen_ref, out_ref, next_ref = refs[:3]
        send_refs = refs[3:]
    else:
        (out_ref,) = refs
    partners = []
    for side in range(6):
        face = jnp.concatenate(split(faces_ref[side ^ 1]), axis=0)
        halo = jnp.concatenate(split(halo_refs[side][...]), axis=0)
        partners.append(dot(own_ref[side], face) + dot(far_ref[side], halo))
    left = iota((ELEMS, 128), 1) < 64
    turned = [[pltpu.roll(p[:, h * 128 : (h + 1) * 128], 64, 1) for h in range(2)] for p in partners]
    joined = []
    for k in range(4):
        h = k // 2
        row = []
        for pair in range(3):
            lower, upper = partners[2 * pair], partners[2 * pair + 1]
            lanes = slice(h * 128, (h + 1) * 128)
            if k % 2 == 0:
                row.append(jnp.where(left, lower[:, lanes], turned[2 * pair + 1][h]))
            else:
                row.append(jnp.where(left, turned[2 * pair][h], upper[:, lanes]))
        joined.append(jnp.concatenate(row, axis=1))
    high, low = split(jnp.concatenate(joined, axis=0))
    select = face_select()
    spread = dot_nt(jnp.concatenate([high, low], axis=0), select)
    spread = spread[: 4 * ELEMS] + spread[4 * ELEMS :]
    state = state_ref[...].reshape(4 * ELEMS, 512)
    tiles = [state[:, t * 128 : (t + 1) * 128] for t in range(4)]
    swapped = [pltpu.roll(tile, 64, 1) for tile in tiles]
    laplace = []
    for s in range(4):
        high, low = split(tiles[s])
        wide = dot(jnp.concatenate([high, low], axis=0), plane_ref[0:128])
        part = wide[: 4 * ELEMS] + wide[4 * ELEMS :] + dot(high, plane_ref[128:256])
        for t in range(4):
            row = 8 * s + 2 * t
            part = part + factor_ref[row : row + 1, :] * tiles[t]
            part = part + factor_ref[row + 1 : row + 2, :] * swapped[t]
        laplace.append(part)
    laplace = jnp.concatenate(laplace, axis=1)
    result = state * keep_ref[...] + viscosity * laplace + penalty * spread
    row = iota((4 * ELEMS, 1), 0)
    result = result + jnp.where(row < 3 * ELEMS, -loading, heating) * force_ref[...]
    out_ref[...] = result.reshape(4, ELEMS, 512)
    if again:
        pick_faces(result, select, chosen_ref, next_ref, send_refs)


def call(kernel, shapes, scratch=(), scalars=0, near=()):
    vmem = pl.BlockSpec(memory_space=pltpu.VMEM)
    smem = pl.BlockSpec(memory_space=pltpu.SMEM)

    def run(*args):
        args = list(args)
        for place in near:
            args[place] = pltpu.with_memory_space_constraint(args[place], pltpu.VMEM)
        return pl.pallas_call(
            kernel,
            out_shape=shapes,
            in_specs=[smem] * scalars + [vmem] * (len(args) - scalars),
            out_specs=jax.tree.map(lambda _: vmem, shapes),
            scratch_shapes=list(scratch),
        )(*args)

    return run


def close(*dims, dtype=f32):
    return pltpu.VMEM(dims, dtype)


def shape(*dims, dtype=f32):
    return jax.ShapeDtypeStruct(dims, dtype)


def local(field, neighbours, cell_one, ref_one, cell_two, ref_two, velocity, rate, cut):
    device = lax.axis_index(("gx", "gy", "gz")).astype(i32).reshape(1)
    near_t = neighbours.T
    plane, factors = laplace_tables()
    plane_high = np.asarray(plane, bf16)
    plane_low = np.asarray(plane - np.asarray(plane_high, np.float64), bf16)
    plane = jnp.asarray(np.concatenate([plane_high, plane_low], axis=0))
    factors = jnp.asarray(factors, f32)
    keep = jnp.asarray(1.0 - penalty * face_table().sum(axis=1), f32)[None]
    row_one, row_two = cell_one[None], cell_two[None]
    slots = close(OWNERS, 4, 128)

    def exchange(block):
        return lax.all_to_all(block, ("gy", "gz"), split_axis=0, concat_axis=0, tiled=True)

    def neighbour_faces(sends):
        arrived = [None] * 6
        for axis_index, axis in enumerate(("gx", "gy", "gz")):
            count = lax.axis_size(axis)
            up = [(i, (i + 1) % count) for i in range(count)]
            arrived[2 * axis_index] = lax.ppermute(sends[2 * axis_index + 1], axis, up)
            arrived[2 * axis_index + 1] = lax.ppermute(
                sends[2 * axis_index], axis, [(b, a) for a, b in up]
            )
        return arrived

    face_shapes = [close(6, ELEMS, 256)] + [close(16, 256)] * 6

    def particles(incoming, state, shift):
        back = slots if shift else close(OWNERS, 2, 128)
        return call(
            functools.partial(particle_kernel, shift),
            [back, close(4 * ELEMS, 512)],
            scratch=[
                pltpu.VMEM((ROWS, 4, 128), f32),
                pltpu.VMEM((ROWS, 4, 128), f32),
                pltpu.VMEM((ROWS + 1, 4, 128), f32),
                pltpu.VMEM((6 * ELEMS, 512), bf16),
                pltpu.VMEM((BODY, 64, CHUNK), f32),
                pltpu.VMEM((BODY, 1024, CHUNK), bf16),
                pltpu.VMEM((BODY, 2, 4 * ELEMS, CHUNK), bf16),
                pltpu.VMEM((512, 4 * ELEMS), f32),
            ],
            near=(0, 1),
        )(incoming, state)

    outgoing, code_rate = call(send_kernel, [slots, shape(2, BIN)])(
        row_one, ref_one, velocity, rate[None]
    )
    incoming = exchange(outgoing)
    owners = lax.axis_size("gy") * lax.axis_size("gz")
    following = lax.ppermute(
        code_rate, ("gy", "gz"), [((i + 1) % owners, i) for i in range(owners)]
    )
    moved = lax.dynamic_slice_in_dim(
        jnp.concatenate([code_rate, following], axis=1), cut[0], BIN, 1
    )
    chosen, faces, *sends = call(
        links_kernel, [shape(6, 16, ELEMS, dtype=bf16)] + face_shapes, scalars=1
    )(device, field, near_t)
    arrived = neighbour_faces(sends)

    incoming, moved = lax.optimization_barrier((incoming, moved))
    back, force = particles(incoming, field, True)
    returned = exchange(back)
    force, near_t, row_two = lax.optimization_barrier((force, near_t, row_two))
    hots = [close(6, ELEMS, 2 * ELEMS, dtype=bf16), close(6, ELEMS, 32, dtype=bf16)]
    code_two, own, far = call(
        tables_kernel, [close(1, BIN, dtype=i32)] + hots, scalars=1, near=(1, 2)
    )(device, near_t, row_two)
    tables = (own, far, plane, factors, keep)
    middle, faces, *sends = call(
        functools.partial(fluid_kernel, True), [close(4, ELEMS, 512)] + face_shapes, near=(1, 2, 3, 7, 8, 9, 10, 11, 12, 13)
    )(field, force, *tables, faces, *arrived, chosen)
    returned, middle, *sends = lax.optimization_barrier((returned, middle, *sends))
    arrived = neighbour_faces(sends)
    outgoing = call(resend_kernel, slots, scalars=1, near=(1, 2, 3, 4, 5))(
        cut, returned, moved, row_two, code_two, ref_two
    )
    incoming = exchange(outgoing)
    back, force = particles(incoming, middle, False)
    returned = exchange(back)
    final_state = call(
        functools.partial(fluid_kernel, False), shape(4, ELEMS, 512), near=(0, 1, 2, 3, 7, 8, 9, 10, 11, 12, 13)
    )(middle, force, *tables, faces, *arrived)
    final_speeds = call(final_kernel, shape(3, BIN), near=(0, 1))(returned, code_two)
    return (final_state, final_speeds)


def solution(mesh):
    in_specs = (
        P(None, ("gx", "gy", "gz"), None),
        P(("gx", "gy", "gz"), None),
        P(("gx", "gy", "gz")),
        P(None, ("gx", "gy", "gz")),
        P(("gx", "gy", "gz")),
        P(None, ("gx", "gy", "gz")),
        P(None, ("gx", "gy", "gz")),
        P(("gx", "gy", "gz")),
        P(),
    )
    out_specs = (P(None, ("gx", "gy", "gz"), None), P(None, ("gx", "gy", "gz")))

    return jax.shard_map(local, mesh=mesh, in_specs=in_specs, out_specs=out_specs, check_vma=False)
```

```python
import functools

import jax
import jax.numpy as jnp
import numpy as np
from jax import lax
from jax.experimental import pallas as pl
from jax.experimental.pallas import tpu as pltpu
from jax.sharding import PartitionSpec as P


node_points = -np.cos(np.pi * np.arange(8) / 7.0)
step_time = 0.1
viscosity = 0.002
penalty = 0.25
loading = 0.5
heating = 0.5

ELEMS = 64
OWNERS = 64
BIN = 2048
CAP = 64
ROWS = OWNERS * CAP // 128
CHUNK_ROWS = 4
CHUNK = 128 * CHUNK_ROWS
BODY = 8

f32 = jnp.float32
bf16 = jnp.bfloat16
i32 = jnp.int32


def second_table():
    differences = node_points[:, None] - node_points[None, :] + np.eye(8)
    weights = 1.0 / np.prod(differences, axis=1)
    derivative = weights[None, :] / weights[:, None] / differences
    derivative = derivative * (1.0 - np.eye(8))
    derivative = derivative - np.eye(8) * derivative.sum(axis=1)[:, None]
    second = derivative @ derivative
    return second


def laplace_tables():
    second = second_table()
    plane = np.kron(second, np.eye(8)) + np.kron(np.eye(8), second)
    factors = np.zeros((32, 128))
    for s in range(4):
        for t in range(4):
            factors[8 * s + 2 * t, :64] = second[2 * s, 2 * t]
            factors[8 * s + 2 * t, 64:] = second[2 * s + 1, 2 * t + 1]
            factors[8 * s + 2 * t + 1, :64] = second[2 * s, 2 * t + 1]
            factors[8 * s + 2 * t + 1, 64:] = second[2 * s + 1, 2 * t]
    return np.kron(np.eye(2), plane).T, factors


def face_table():
    selection = np.zeros((512, 384))
    for face_side in range(6):
        edge_value = 0 if face_side % 2 == 0 else 7
        for row_node in range(8):
            for col_node in range(8):
                if face_side < 2:
                    node_index = (edge_value * 8 + row_node) * 8 + col_node
                elif face_side < 4:
                    node_index = (row_node * 8 + edge_value) * 8 + col_node
                else:
                    node_index = (row_node * 8 + col_node) * 8 + edge_value
                selection[node_index, face_side * 64 + row_node * 8 + col_node] = 1.0
    return selection


def face_select():
    col = iota((1, 384), 1)
    side, first, second = col >> 6, (col >> 3) & 7, col & 7
    edge = (side & 1) * 7
    node_a = edge * 64 + first * 8 + second
    node_b = first * 64 + edge * 8 + second
    node_c = first * 64 + second * 8 + edge
    node = jnp.where(side < 2, node_a, jnp.where(side < 4, node_b, node_c))
    return jnp.where(iota((512, 384), 0) == node, 1.0, 0.0).astype(bf16)


def iota(shape, axis):
    return lax.broadcasted_iota(i32, shape, axis)


def split(x):
    high = x.astype(bf16)
    return high, (x - high.astype(f32)).astype(bf16)


def split_row(x):
    high = x.astype(bf16).astype(f32)
    return high, x - high


def dot(a, b):
    return jnp.dot(a, b, preferred_element_type=f32)


def dot_nt(a, b):
    return lax.dot_general(a, b, (((1,), (1,)), ((), ())), preferred_element_type=f32)


def rank_in_owner(owner):
    width = 256
    upto = jnp.where(iota((width, width), 0) <= iota((width, width), 1), 1.0, 0.0).astype(bf16)
    table = jnp.concatenate([upto, jnp.ones((width, width), bf16)], axis=0)
    before = jnp.zeros((OWNERS, width), f32)
    ranks = []
    for start in range(0, BIN, width):
        here = iota((OWNERS, width), 0) == owner[:, start : start + width]
        marks = jnp.where(here, 1.0, 0.0)
        counts = dot(jnp.concatenate([marks, before], axis=1).astype(bf16), table)
        ranks.append(jnp.sum(jnp.where(here, counts, 0.0), axis=0, keepdims=True) - 1.0)
        before = before + marks
    return jnp.concatenate(ranks, axis=1)


def thick(row, rows):
    sixteen = jnp.broadcast_to(row, (16, row.shape[1])).astype(bf16)
    return jnp.concatenate([sixteen] * (rows // 16), axis=0)


def one_hot(index, rows):
    return jnp.where(iota((rows, index.shape[1]), 0) == index, 1.0, 0.0).astype(bf16)


def scatter_slots(out_ref, owner, rank, values):
    owned = one_hot(owner, OWNERS)
    placed = one_hot(rank, CAP)
    for first in range(0, len(values), 4):
        highs, lows = [], []
        for value in values[first : first + 4]:
            high, low = split_row(value)
            highs.append(placed * thick(high, CAP))
            lows.append(placed * thick(low, CAP))
        out = dot_nt(owned, jnp.concatenate(highs, axis=0)) + dot_nt(
            owned, jnp.concatenate(lows, axis=0)
        )
        out_ref[:, first // 2, :] = out[:, :128]
        out_ref[:, first // 2 + 1, :] = out[:, 128:]


def gather_slots(blocks, owner, lane_hot):
    high, low = split(jnp.concatenate(blocks, axis=0))
    total = dot(jnp.concatenate([high, low], axis=1), jnp.concatenate([lane_hot] * 2, axis=0))
    owned = iota((OWNERS, BIN), 0) == owner
    return [
        jnp.sum(jnp.where(owned, total[k * OWNERS : (k + 1) * OWNERS], 0.0), axis=0, keepdims=True)
        for k in range(len(blocks))
    ]


def send_kernel(cell_ref, coord_ref, speed_ref, rate_ref, out_ref, code_ref):
    cell = cell_ref[...]
    owner = (cell >> 6) & (OWNERS - 1)
    element = (cell & (ELEMS - 1)).astype(f32)
    rank = rank_in_owner(owner)
    code_ref[0:1, :] = owner.astype(f32) * float(CAP) + rank
    code_ref[1:2, :] = rate_ref[...]
    values = [
        element,
        speed_ref[0:1, :],
        coord_ref[0:1, :],
        speed_ref[1:2, :],
        coord_ref[1:2, :],
        speed_ref[2:3, :],
        coord_ref[2:3, :],
        rate_ref[...],
    ]
    scatter_slots(out_ref, owner, rank.astype(i32), values)


def known_kernel(moved_ref, cell_ref, code_ref, coord_ref, out_ref):
    code = code_ref[...]
    element = (cell_ref[...] & (ELEMS - 1)).astype(f32)
    zero = jnp.zeros((1, BIN), f32)
    values = [element, zero, coord_ref[0:1, :], zero, coord_ref[1:2, :], zero, coord_ref[2:3, :], moved_ref[1:2, :]]
    scatter_slots(out_ref, code >> 6, code & (CAP - 1), values)


def resend_kernel(cut_ref, back_ref, moved_ref, known_ref, code_ref, out_ref):
    first_code = moved_ref[0:1, :].astype(i32)
    part = jnp.where(iota((1, BIN), 1) + cut_ref[0] >= BIN, CAP, 0)
    lane_hot = one_hot((first_code & (CAP - 1)) + part, 128)
    speeds = gather_slots([back_ref[:, k, :] for k in range(3)], first_code >> 6, lane_hot)
    code = code_ref[...]
    owned = one_hot(code >> 6, OWNERS)
    placed = one_hot(code & (CAP - 1), CAP)
    empty = jnp.zeros((CAP, BIN), bf16)
    highs, lows = [], []
    for k in range(3):
        high, low = split_row(speeds[k])
        highs.append(placed * thick(high, CAP))
        lows.append(placed * thick(low, CAP))
    out = dot_nt(owned, jnp.concatenate([highs[1], highs[0], empty, highs[2]], axis=0)) + dot_nt(
        owned, jnp.concatenate([lows[1], lows[0], empty, lows[2]], axis=0)
    )
    left = iota((OWNERS, 128), 1) < 64
    pair, last = out[:, :128], out[:, 128:]
    for j, speed in enumerate((pair, pltpu.roll(pair, 64, 1), last)):
        out_ref[:, j, :] = jnp.where(left, known_ref[:, j, :], speed)
    out_ref[:, 3, :] = known_ref[:, 3, :]


def final_kernel(back_ref, code_ref, out_ref):
    code = code_ref[...]
    lane_hot = jnp.concatenate([one_hot(code & (CAP - 1), CAP)] * 2, axis=0)
    left = iota((OWNERS, 128), 1) < 64
    pair, last = back_ref[:, 0, :], back_ref[:, 1, :]
    blocks = [jnp.where(left, pair, 0.0), jnp.where(left, 0.0, pair), jnp.where(left, last, 0.0)]
    speeds = gather_slots(blocks, code >> 6, lane_hot)
    for k in range(3):
        out_ref[k : k + 1, :] = speeds[k]


def column(values):
    row = iota((8, 1), 0)
    result = jnp.zeros((8, 1), f32)
    for index, value in enumerate(values):
        result = jnp.where(row == index, float(value), result)
    return result


def lagrange(x):
    gaps = node_points[:, None] - node_points[None, :] + np.eye(8)
    one = pltpu.roll(x - column(node_points), 1, 0)
    two = one * pltpu.roll(one, 1, 0)
    four = two * pltpu.roll(two, 2, 0)
    last = pltpu.roll(one, 6, 0) * column(1.0 / np.prod(gaps, axis=1))
    return four * pltpu.roll(two, 4, 0) * last


def basis(coords, pair_ref, weight_ref):
    first, second, third = [lagrange(x) for x in coords]
    for a in range(8):
        pair_ref[8 * a : 8 * a + 8, :] = first[a : a + 1, :] * second
    for i in range(32):
        piece = jnp.concatenate(
            [pair_ref[2 * i + h : 2 * i + h + 1, :] * third for h in range(2)], axis=0
        )
        weight_ref[16 * i : 16 * i + 16, :], weight_ref[512 + 16 * i : 528 + 16 * i, :] = split(piece)


def along(rows, k):
    return jnp.concatenate([rows[i, k : k + 1, :] for i in range(CHUNK_ROWS)], axis=1)


def particle_kernel(shift, incoming_ref, state_ref, back_ref, force_ref, even_ref, odd_ref, fresh_ref, state_scr, pair_refs, weight_refs, source_refs, total_ref):
    low, high = incoming_ref[0:ROWS], incoming_ref[ROWS : 2 * ROWS]
    left = iota(low.shape, 2) < 64
    even_ref[...] = jnp.where(left, low, pltpu.roll(high, 64, 2))
    odd_ref[...] = jnp.where(left, pltpu.roll(low, 64, 2), high)
    high, low = split(state_ref[0:3].reshape(3 * ELEMS, 512))
    state_scr[0 : 3 * ELEMS] = high
    state_scr[3 * ELEMS :] = low
    fresh_ref[:, 3:4, :] = jnp.zeros((ROWS + 1, 1, 128), f32)

    total_ref[...] = jnp.zeros_like(total_ref)

    def one(start, weight_ref, source_ref, pair_ref):
        even = even_ref[pl.ds(start, CHUNK_ROWS)]
        odd = odd_ref[pl.ds(start, CHUNK_ROWS)]
        basis([along(even, k) for k in (1, 2, 3)], pair_ref, weight_ref)
        wide = dot(state_scr[...], weight_ref[0:512])
        rest = dot(state_scr[0 : 3 * ELEMS], weight_ref[512:1024])
        element = along(even, 0).astype(i32)
        here = iota((ELEMS, CHUNK), 0) == element
        rates = along(odd, 3)
        squares = None
        fresh, sources = [], []
        for k in range(3):
            rows = slice(k * ELEMS, (k + 1) * ELEMS)
            lower = slice((k + 3) * ELEMS, (k + 4) * ELEMS)
            picked = jnp.where(here, wide[rows] + wide[lower] + rest[rows], 0.0)
            speed = along(odd, k)
            offset = jnp.sum(picked, axis=0, keepdims=True) - speed
            accel = rates * offset
            squares = offset * offset if squares is None else squares + offset * offset
            sources.append(accel)
            fresh.append(speed + step_time * accel)
        sources.append(rates * squares)
        for i in range(CHUNK_ROWS):
            for k in range(3):
                fresh_ref[start + i, k : k + 1, :] = fresh[k][:, i * 128 : (i + 1) * 128]
        hot = one_hot(element, ELEMS)
        for k in range(4):
            high, low = split_row(sources[k])
            source_ref[0, k * ELEMS : (k + 1) * ELEMS] = hot * thick(high, ELEMS)
            source_ref[1, k * ELEMS : (k + 1) * ELEMS] = hot * thick(low, ELEMS)

    def push(weight_ref, source_ref):
        wide = dot_nt(weight_ref[...], source_ref[0])
        total_ref[...] += wide[:512] + wide[512:] + dot_nt(weight_ref[0:512], source_ref[1])

    def visit(index, carry):
        for h in range(BODY):
            one((index * BODY + h) * CHUNK_ROWS, weight_refs.at[h], source_refs.at[h], pair_refs.at[h])
        for h in range(BODY):
            push(weight_refs.at[h], source_refs.at[h])
        return carry

    lax.fori_loop(0, ROWS // CHUNK_ROWS // BODY, visit, 0)
    fresh = fresh_ref[0:ROWS]
    if shift:
        fresh_ref[ROWS] = pltpu.roll(fresh_ref[0], 64, 1)
        after = fresh_ref[1 : ROWS + 1]
        left = iota(fresh.shape, 2) < 64
        back_ref[0:ROWS] = jnp.where(left, fresh, pltpu.roll(after, 64, 2))
        back_ref[ROWS : 2 * ROWS] = jnp.where(left, pltpu.roll(fresh, 64, 2), after)
    else:
        turned = pltpu.roll(fresh, 64, 2)
        left = iota((ROWS, 1, 128), 2) < 64
        back_ref[0:ROWS, 0:1, :] = jnp.where(left, fresh[:, 0:1, :], turned[:, 1:2, :])
        back_ref[0:ROWS, 1:2, :] = fresh[:, 2:3, :]
        back_ref[ROWS : 2 * ROWS, 0:1, :] = jnp.where(left, turned[:, 0:1, :], fresh[:, 1:2, :])
        back_ref[ROWS : 2 * ROWS, 1:2, :] = turned[:, 2:3, :]
    force_ref[...] = total_ref[...].T


def pick_faces(state, select, chosen_ref, faces_ref, send_refs):
    high, low = split(state)
    picked = dot(jnp.concatenate([high, low], axis=0), select)
    picked = picked[: 4 * ELEMS] + picked[4 * ELEMS :]
    left = iota((ELEMS, 128), 1) < 64
    for pair in range(3):
        tiles = [picked[k * ELEMS : (k + 1) * ELEMS, pair * 128 : (pair + 1) * 128] for k in range(4)]
        turned = [pltpu.roll(tile, 64, 1) for tile in tiles]
        lower = [jnp.where(left, tiles[k], turned[k + 1]) for k in (0, 2)]
        upper = [jnp.where(left, turned[k], tiles[k + 1]) for k in (0, 2)]
        for side, parts in ((2 * pair, lower), (2 * pair + 1, upper)):
            face = jnp.concatenate(parts, axis=1)
            faces_ref[side] = face
            face_high, face_low = split(face)
            send_refs[side][...] = dot(chosen_ref[side], face_high) + dot(chosen_ref[side], face_low)


def links_kernel(device_ref, state_ref, near_t_ref, chosen_ref, faces_ref, *send_refs):
    device = device_ref[0]
    near_t = near_t_ref[...].astype(f32)
    near = jnp.concatenate([near_t, near_t[0:2]], axis=0).T.astype(i32)
    for side in range(6):
        outside = (near[:, side : side + 1] >> 6) != device
        outside_t = (near_t_ref[side : side + 1, :] >> 6) != device
        before = (iota((ELEMS, ELEMS), 0) < iota((ELEMS, ELEMS), 1)) & outside
        rank = jnp.sum(jnp.where(before, 1.0, 0.0), axis=0, keepdims=True)
        rank = jnp.where(outside_t, rank, -1.0)
        chosen = iota((16, ELEMS), 0).astype(f32) == rank
        chosen_ref[side] = jnp.where(chosen, 1.0, 0.0).astype(bf16)
    pick_faces(state_ref[...].reshape(4 * ELEMS, 512), face_select(), chosen_ref, faces_ref, send_refs)


def tables_kernel(device_ref, near_t_ref, cell_ref, code_ref, own_ref, far_ref):
    device = device_ref[0]
    near_t = near_t_ref[...].astype(f32)
    near = jnp.concatenate([near_t, near_t[0:2]], axis=0).T.astype(i32)
    for side in range(6):
        target = near[:, side : side + 1]
        target_t = near_t_ref[side : side + 1, :]
        outside = (target >> 6) != device
        remote = (target >= 0) & outside
        remote_t = (target_t >= 0) & ((target_t >> 6) != device)
        slot = jnp.where(outside, -1, target & (ELEMS - 1))
        own = (iota((ELEMS, 2 * ELEMS), 1) & (ELEMS - 1)) == slot
        own_ref[side] = jnp.where(own, 1.0, 0.0).astype(bf16)
        key = jnp.where(remote, target & (ELEMS - 1), ELEMS)
        key_t = jnp.where(remote_t, target_t & (ELEMS - 1), ELEMS)
        rank = jnp.sum(jnp.where(key_t < key, 1.0, 0.0), axis=1, keepdims=True)
        rank = jnp.where(remote, rank, -1.0)
        far = (iota((ELEMS, 32), 1) & 15).astype(f32) == rank
        far_ref[side] = jnp.where(far, 1.0, 0.0).astype(bf16)
    owner = (cell_ref[...] >> 6) & (OWNERS - 1)
    code_ref[...] = owner * CAP + rank_in_owner(owner).astype(i32)


def fluid_kernel(again, state_ref, force_ref, own_ref, far_ref, plane_ref, factor_ref, keep_ref, faces_ref, *refs):
    halo_refs, refs = refs[:6], refs[6:]
    if again:
        chosen_ref, out_ref, next_ref = refs[:3]
        send_refs = refs[3:]
    else:
        (out_ref,) = refs
    partners = []
    for side in range(6):
        face = jnp.concatenate(split(faces_ref[side ^ 1]), axis=0)
        halo = jnp.concatenate(split(halo_refs[side][...]), axis=0)
        partners.append(dot(own_ref[side], face) + dot(far_ref[side], halo))
    left = iota((ELEMS, 128), 1) < 64
    turned = [[pltpu.roll(p[:, h * 128 : (h + 1) * 128], 64, 1) for h in range(2)] for p in partners]
    joined = []
    for k in range(4):
        h = k // 2
        row = []
        for pair in range(3):
            lower, upper = partners[2 * pair], partners[2 * pair + 1]
            lanes = slice(h * 128, (h + 1) * 128)
            if k % 2 == 0:
                row.append(jnp.where(left, lower[:, lanes], turned[2 * pair + 1][h]))
            else:
                row.append(jnp.where(left, turned[2 * pair][h], upper[:, lanes]))
        joined.append(jnp.concatenate(row, axis=1))
    high, low = split(jnp.concatenate(joined, axis=0))
    select = face_select()
    spread = dot_nt(jnp.concatenate([high, low], axis=0), select)
    spread = spread[: 4 * ELEMS] + spread[4 * ELEMS :]
    state = state_ref[...].reshape(4 * ELEMS, 512)
    tiles = [state[:, t * 128 : (t + 1) * 128] for t in range(4)]
    swapped = [pltpu.roll(tile, 64, 1) for tile in tiles]
    laplace = []
    for s in range(4):
        high, low = split(tiles[s])
        wide = dot(jnp.concatenate([high, low], axis=0), plane_ref[0:128])
        part = wide[: 4 * ELEMS] + wide[4 * ELEMS :] + dot(high, plane_ref[128:256])
        for t in range(4):
            row = 8 * s + 2 * t
            part = part + factor_ref[row : row + 1, :] * tiles[t]
            part = part + factor_ref[row + 1 : row + 2, :] * swapped[t]
        laplace.append(part)
    laplace = jnp.concatenate(laplace, axis=1)
    result = state * keep_ref[...] + viscosity * laplace + penalty * spread
    row = iota((4 * ELEMS, 1), 0)
    result = result + jnp.where(row < 3 * ELEMS, -loading, heating) * force_ref[...]
    out_ref[...] = result.reshape(4, ELEMS, 512)
    if again:
        pick_faces(result, select, chosen_ref, next_ref, send_refs)


def call(kernel, shapes, scratch=(), scalars=0, near=()):
    vmem = pl.BlockSpec(memory_space=pltpu.VMEM)
    smem = pl.BlockSpec(memory_space=pltpu.SMEM)

    def run(*args):
        args = list(args)
        for place in near:
            args[place] = pltpu.with_memory_space_constraint(args[place], pltpu.VMEM)
        return pl.pallas_call(
            kernel,
            out_shape=shapes,
            in_specs=[smem] * scalars + [vmem] * (len(args) - scalars),
            out_specs=jax.tree.map(lambda _: vmem, shapes),
            scratch_shapes=list(scratch),
        )(*args)

    return run


def close(*dims, dtype=f32):
    return pltpu.VMEM(dims, dtype)


def shape(*dims, dtype=f32):
    return jax.ShapeDtypeStruct(dims, dtype)


def local(field, neighbours, cell_one, ref_one, cell_two, ref_two, velocity, rate, cut):
    device = lax.axis_index(("gx", "gy", "gz")).astype(i32).reshape(1)
    near_t = neighbours.T
    plane, factors = laplace_tables()
    plane_high = np.asarray(plane, bf16)
    plane_low = np.asarray(plane - np.asarray(plane_high, np.float64), bf16)
    plane = jnp.asarray(np.concatenate([plane_high, plane_low], axis=0))
    factors = jnp.asarray(factors, f32)
    keep = jnp.asarray(1.0 - penalty * face_table().sum(axis=1), f32)[None]
    row_one, row_two = cell_one[None], cell_two[None]
    slots = close(OWNERS, 4, 128)

    def exchange(block):
        return lax.all_to_all(block, ("gy", "gz"), split_axis=0, concat_axis=0, tiled=True)

    def neighbour_faces(sends):
        arrived = [None] * 6
        for axis_index, axis in enumerate(("gx", "gy", "gz")):
            count = lax.axis_size(axis)
            up = [(i, (i + 1) % count) for i in range(count)]
            arrived[2 * axis_index] = lax.ppermute(sends[2 * axis_index + 1], axis, up)
            arrived[2 * axis_index + 1] = lax.ppermute(
                sends[2 * axis_index], axis, [(b, a) for a, b in up]
            )
        return arrived

    face_shapes = [close(6, ELEMS, 256)] + [close(16, 256)] * 6

    def particles(incoming, state, shift):
        back = slots if shift else close(OWNERS, 2, 128)
        return call(
            functools.partial(particle_kernel, shift),
            [back, close(4 * ELEMS, 512)],
            scratch=[
                pltpu.VMEM((ROWS, 4, 128), f32),
                pltpu.VMEM((ROWS, 4, 128), f32),
                pltpu.VMEM((ROWS + 1, 4, 128), f32),
                pltpu.VMEM((6 * ELEMS, 512), bf16),
                pltpu.VMEM((BODY, 64, CHUNK), f32),
                pltpu.VMEM((BODY, 1024, CHUNK), bf16),
                pltpu.VMEM((BODY, 2, 4 * ELEMS, CHUNK), bf16),
                pltpu.VMEM((512, 4 * ELEMS), f32),
            ],
            near=(0, 1),
        )(incoming, state)

    outgoing, code_rate = call(send_kernel, [slots, shape(2, BIN)])(
        row_one, ref_one, velocity, rate[None]
    )
    incoming = exchange(outgoing)
    owners = lax.axis_size("gy") * lax.axis_size("gz")
    following = lax.ppermute(
        code_rate, ("gy", "gz"), [((i + 1) % owners, i) for i in range(owners)]
    )
    moved = lax.dynamic_slice_in_dim(
        jnp.concatenate([code_rate, following], axis=1), cut[0], BIN, 1
    )
    chosen, faces, *sends = call(
        links_kernel, [shape(6, 16, ELEMS, dtype=bf16)] + face_shapes, scalars=1
    )(device, field, near_t)
    arrived = neighbour_faces(sends)

    incoming, moved = lax.optimization_barrier((incoming, moved))
    back, force = particles(incoming, field, True)
    returned = exchange(back)
    force, near_t, row_two = lax.optimization_barrier((force, near_t, row_two))
    hots = [close(6, ELEMS, 2 * ELEMS, dtype=bf16), close(6, ELEMS, 32, dtype=bf16)]
    code_two, own, far = call(
        tables_kernel, [close(1, BIN, dtype=i32)] + hots, scalars=1, near=(1, 2)
    )(device, near_t, row_two)
    known = call(known_kernel, slots, near=(0, 1, 2, 3))(
        moved, row_two, code_two, ref_two
    )
    tables = (own, far, plane, factors, keep)
    middle, faces, *sends = call(
        functools.partial(fluid_kernel, True), [close(4, ELEMS, 512)] + face_shapes, near=(1, 2, 3, 7, 8, 9, 10, 11, 12, 13)
    )(field, force, *tables, faces, *arrived, chosen)
    returned, middle, known, *sends = lax.optimization_barrier((returned, middle, known, *sends))
    arrived = neighbour_faces(sends)
    outgoing = call(resend_kernel, slots, scalars=1, near=(1, 2, 3, 4))(cut, returned, moved, known, code_two)
    incoming = exchange(outgoing)
    back, force = particles(incoming, middle, False)
    returned = exchange(back)
    final_state = call(
        functools.partial(fluid_kernel, False), shape(4, ELEMS, 512), near=(0, 1, 2, 3, 7, 8, 9, 10, 11, 12, 13)
    )(middle, force, *tables, faces, *arrived)
    final_speeds = call(final_kernel, shape(3, BIN), near=(0, 1))(returned, code_two)
    return (final_state, final_speeds)


def solution(mesh):
    in_specs = (
        P(None, ("gx", "gy", "gz"), None),
        P(("gx", "gy", "gz"), None),
        P(("gx", "gy", "gz")),
        P(None, ("gx", "gy", "gz")),
        P(("gx", "gy", "gz")),
        P(None, ("gx", "gy", "gz")),
        P(None, ("gx", "gy", "gz")),
        P(("gx", "gy", "gz")),
        P(),
    )
    out_specs = (P(None, ("gx", "gy", "gz"), None), P(None, ("gx", "gy", "gz")))

    return jax.shard_map(local, mesh=mesh, in_specs=in_specs, out_specs=out_specs, check_vma=False)
```
